128 devices in a mesh: ma: 4 (over y), mb: 32 (over x, z, core).
Axes of the slice: x: 4, y: 4, z: 4, core: 2. Of those that a mesh axis runs over, the one named last changes fastest.
Arguments:
- tier_four: float32 [1024, 2, 128, 128], P(('ma', 'mb')), may hold values from -6 to 6
- tier_six: float32 [1024, 2, 128, 128], P(('ma', 'mb')), may hold values from -6 to 6
- tier_seven: float32 [1024, 2, 128, 128], P(('ma', 'mb')), may hold values from -6 to 6
- coupling: float32 [128, 128], replicated
- eigenbasis: float32 [128, 128], replicated
- energies: float32 [128], replicated, may hold values from -6 to 6
- decay_rates: float32 [12], replicated, may hold values from 0.5 to 4
- bath_coefficients: float32 [2, 12], replicated, may hold values from -1 to 1
- occupation_five: int32 [1024, 12], P(('ma', 'mb')), may hold values from 0 to 5, as said below
- local_five: int32 [1024, 2, 9], P(('ma', 'mb')), may hold values from 0 to 7
- peers_five: int32 [1024, 4], P(('ma', 'mb')), may hold values from 0 to 31, all different within a row; in each aligned block of 8 rows (0 to 7, 8 to 15, ...) at most 2 rows name the same one
- places_five: int32 [1024, 4], P(('ma', 'mb')), may hold values from 0 to 7
- occupation_six: int32 [1024, 12], P(('ma', 'mb')), may hold values from 0 to 6, as said below
- local_six: int32 [1024, 2, 9], P(('ma', 'mb')), may hold values from 0 to 7
- peers_six: int32 [1024, 4], P(('ma', 'mb')), may hold values from 0 to 31, all different within a row; in each aligned block of 8 rows (0 to 7, 8 to 15, ...) at most 2 rows name the same one
- places_six: int32 [1024, 4], P(('ma', 'mb')), may hold values from 0 to 7
Outputs:
- updated_five: float32 [1024, 2, 128, 128], P(('ma', 'mb'))
- updated_six: float32 [1024, 2, 128, 128], P(('ma', 'mb'))
The draws below stay inside these ranges and needn't reach their ends.
Inputs may be any that keep to these rules, and one draw needn't show every extreme that they name: `occupation_five`: each row sums to 5; the first row of every block of 8 rows has all 5 in one mode. `occupation_six`: each row sums to 6; the first row of every block of 8 rows has all 6 in one mode. `local_five`: positions within the matrix's own block of 8 rows; a lowered entry is read only where its mode's occupation is positive. `local_six`: positions within the matrix's own block of 8 rows; a lowered entry is read only where its mode's occupation is positive. `peers_five`: the four entries of a row differ; among the rows of one block of 8 rows no value appears more than 2 times, and some value appears exactly 2 times. `peers_six`: the four entries of a row differ; among the rows of one block of 8 rows no value appears more than 2 times, and some value appears exactly 2 times.
All inputs are finite; a program needn't handle non-finite values.
Results may differ from the reference program's by a relative error of at most 0.0003.
Values sent between devices are 32-bit elements; how exact they have to be, the bound alone decides.
A program may use at most 128 MiB of HBM per device.

```python
import math
import jax
import jax.numpy as jnp
import numpy as np
from jax import lax

NB = 128
K = 12
M_DEV = 8
CAP = 2
M_ALL = 1024
LOCAL_MODES = 9
N_MA = 4
N_MB = 32


def occupations(key, tier_count):
    picks = jax.random.randint(key, (M_ALL, tier_count), 0, K)
    leading = jnp.arange(M_ALL, dtype=jnp.int32)[:, None] % M_DEV == 0
    picks = jnp.where(leading, picks[:, :1], picks)
    return jnp.sum((picks[:, :, None] == jnp.arange(K, dtype=jnp.int32)[None, None, :]).astype(jnp.int32), axis=1)


def draw_occupation_five(key, part):
    return occupations(jax.random.fold_in(key, 41), 5)


def draw_occupation_six(key, part):
    return occupations(jax.random.fold_in(key, 53), 6)


def draw_coupling(key, part):
    raw_entries = jax.random.normal(jax.random.fold_in(key, 7), (NB, NB), jnp.float32)
    return (raw_entries + jnp.transpose(raw_entries)) / jnp.sqrt(2.0 * NB)


def draw_eigenbasis(key, part):
    mirrors = jax.random.normal(jax.random.fold_in(key, 11), (NB, NB), jnp.float32)

    def reflect(turn_index, frames):
        mirror = mirrors[turn_index]
        image_vec = jnp.dot(frames, mirror, precision=lax.Precision.HIGHEST)
        return frames - 2.0 * jnp.outer(image_vec, mirror) / jnp.sum(mirror * mirror)
    return lax.fori_loop(0, NB, reflect, jnp.eye(NB, dtype=jnp.float32))


def set_ends(array, stream_key, least, largest):
    longest = array.shape.index(max(array.shape))
    spots = []
    for shift in (0, 1):
        where = [jax.random.randint(jax.random.fold_in(stream_key, axis), (), 0, length) for axis, length in enumerate(array.shape)]
        where[longest] = (where[longest] + shift) % array.shape[longest]
        spots.append(tuple(where))
    return array.at[spots[0]].set(least).at[spots[1]].set(largest)


def block_scale(key, dims, cuts, least, top_value):
    gain, own = 1.0, jax.random.fold_in(key, 6)
    for dim, shards_of in cuts:
        draws = jnp.exp(jax.random.uniform(jax.random.fold_in(own, dim), (shards_of,), jnp.float32, least / len(cuts), top_value / len(cuts)))
        gain = gain * jnp.repeat(draws, dims[dim] // shards_of).reshape([-1 if axis == dim else 1 for axis in range(len(dims))])
    return gain


def shared_out(key, own, number, rows, count, top, reach, lean):
    order = jax.random.permutation(key, count)
    packed, common = load_shares(count, rows * top, reach, lean, True), load_shares(count, rows * top, reach, lean, False)
    places = jnp.arange(count)

    def named(tallies, turn):
        used = int((tallies > 0).sum())
        fixed = max(1, used // 4)
        shifted = fixed + (places - fixed + turn * (used - fixed)) % max(1, count - fixed)
        return jnp.zeros((count,), jnp.int32).at[order[jnp.where(places < fixed, places, shifted)]].set(jnp.asarray(tallies, jnp.int32))

    tallies = jnp.where(number % 4 == 0, named(packed, number // 4), named(common, number - number // 4 - 1))
    mixed = jax.random.permutation(jax.random.fold_in(own, 3), count)
    giver, taker = mixed[0:count // 2 * 2:2], mixed[1:count // 2 * 2:2]
    slack = jnp.minimum(tallies[giver] - 1, reach - tallies[taker]) // 2
    slack = jnp.where((giver == order[0]) | (taker == order[0]) | (tallies[taker] == 0), 0, jnp.maximum(slack, 0))
    shifted = jax.random.randint(jax.random.fold_in(own, 4), (count // 2,), 0, 1 << 20) % (slack + 1)
    tallies = tallies.at[giver].add(-shifted).at[taker].add(shifted)
    items = jnp.searchsorted(jnp.cumsum(tallies), jnp.arange(rows * top), side="right").astype(jnp.int32)
    listing = items.reshape(top, rows).T
    listing = listing[jax.random.permutation(jax.random.fold_in(own, 1), rows)]
    turn = jax.random.randint(jax.random.fold_in(own, 2), (rows, 1), 0, top)
    return jnp.take_along_axis(listing, (jnp.arange(top)[None, :] + turn) % top, axis=1)


def load_shares(number_of, total, reach, lean, full):
    weights = [(1 << 20) // math.isqrt(grade ** lean) + 1 for grade in range(1, number_of + 1)]
    largest = reach if full else min(reach, max(-(-total // number_of), total * weights[0] // sum(weights)))
    least = 1 if total - largest >= number_of - 1 else 0
    holding, surplus = [largest] + [least] * (number_of - 1), total - largest - least * (number_of - 1)
    while surplus > 0:
        candidates = [i for i in range(1, number_of) if holding[i] < largest] or [i for i in range(1, number_of) if holding[i] < reach]
        mass, remaining = sum([weights[i] for i in candidates]), surplus
        for i in candidates:
            extra = min(reach - holding[i], max(1, remaining * weights[i] // mass), surplus)
            holding[i] = holding[i] + extra
            surplus = surplus - extra
    return np.array(holding)


def scatter_about(rng, shape, scale, limit, cuts=(), kind=jnp.bfloat16):
    array = jax.random.normal(rng, shape, jnp.float32) * scale
    if len(cuts) > 0:
        array = block_scale(rng, shape, cuts, -0.22, 0.18) * array
    return jnp.clip(array, min=-limit, max=limit).astype(kind)


def setup_inputs(seed: int = 0) -> dict:
    arg_keys = jax.random.split(jax.random.key(seed), 17)
    tier_four = scatter_about(arg_keys[0], (M_ALL, 2, NB, NB), 1.0, 6.0, ((0, 128),), jnp.float32)
    tier_six = scatter_about(arg_keys[1], (M_ALL, 2, NB, NB), 1.0, 6.0, ((0, 128),), jnp.float32)
    tier_seven = scatter_about(arg_keys[2], (M_ALL, 2, NB, NB), 1.0, 6.0, ((0, 128),), jnp.float32)
    coupling = draw_coupling(jax.random.fold_in(arg_keys[16], 71), 0)
    eigenbasis = draw_eigenbasis(jax.random.fold_in(arg_keys[16], 71), 0)
    energies = jnp.clip(jax.random.uniform(arg_keys[5], (NB,), jnp.float32, -6.0, 6.0), -6.0, 6.0)
    decay_rates = jnp.clip(jnp.exp(jax.random.uniform(arg_keys[6], (K,), jnp.float32, math.log(0.5), math.log(4.0))), 0.5, 4.0)
    bath_coefficients = jnp.clip(jax.random.uniform(arg_keys[7], (2, K), jnp.float32, -1.0, 1.0), -1.0, 1.0)
    occupation_five = draw_occupation_five(jax.random.fold_in(arg_keys[16], 71), 0)
    local_five = set_ends(jax.random.randint(arg_keys[9], (M_ALL, 2, LOCAL_MODES), 0, M_DEV), jax.random.fold_in(arg_keys[9], 1), 0, M_DEV - 1).astype(jnp.int32)
    peers_five_keys = jax.random.split(jax.random.fold_in(arg_keys[10], 1), M_ALL // M_DEV)
    peers_five_turns = jax.random.permutation(jax.random.fold_in(arg_keys[10], 3), M_ALL // M_DEV)
    peers_five = jax.vmap(lambda own, number: shared_out(jax.random.fold_in(arg_keys[10], 2), own, number, M_DEV, N_MB, 4, CAP, 2))(peers_five_keys, peers_five_turns).reshape((M_ALL, 4))
    places_five = set_ends(jax.random.randint(arg_keys[11], (M_ALL, 4), 0, M_DEV), jax.random.fold_in(arg_keys[11], 1), 0, M_DEV - 1).astype(jnp.int32)
    occupation_six = draw_occupation_six(jax.random.fold_in(arg_keys[16], 71), 0)
    local_six = set_ends(jax.random.randint(arg_keys[13], (M_ALL, 2, LOCAL_MODES), 0, M_DEV), jax.random.fold_in(arg_keys[13], 1), 0, M_DEV - 1).astype(jnp.int32)
    peers_six_keys = jax.random.split(jax.random.fold_in(arg_keys[14], 1), M_ALL // M_DEV)
    peers_six_turns = jax.random.permutation(jax.random.fold_in(arg_keys[14], 3), M_ALL // M_DEV)
    peers_six = jax.vmap(lambda own, number: shared_out(jax.random.fold_in(arg_keys[14], 2), own, number, M_DEV, N_MB, 4, CAP, 2))(peers_six_keys, peers_six_turns).reshape((M_ALL, 4))
    places_six = set_ends(jax.random.randint(arg_keys[15], (M_ALL, 4), 0, M_DEV), jax.random.fold_in(arg_keys[15], 1), 0, M_DEV - 1).astype(jnp.int32)
    return dict(tier_four=tier_four, tier_six=tier_six, tier_seven=tier_seven, coupling=coupling, eigenbasis=eigenbasis, energies=energies, decay_rates=decay_rates, bath_coefficients=bath_coefficients, occupation_five=occupation_five, local_five=local_five, peers_five=peers_five, places_five=places_five, occupation_six=occupation_six, local_six=local_six, peers_six=peers_six, places_six=places_six)


HIGHEST = lax.Precision.HIGHEST


def left_product(matrix, batch):
    return jnp.einsum('ij,mjk->mik', matrix, batch, precision=HIGHEST)


def right_product(batch, matrix):
    return jnp.einsum('mij,jk->mik', batch, matrix, precision=HIGHEST)


def mix_terms(up_real, up_imag, sum_rr, sum_ri, sum_ir, sum_ii):
    return (up_real + sum_rr - sum_ii, up_imag + sum_ri + sum_ir,
            up_real + sum_rr + sum_ii, up_imag + sum_ri - sum_ir)


def settle(pair_real, pair_imag, other_real, other_imag, occupation, coupling, eigenbasis, energies, decay_rates):
    comm_real = left_product(coupling, pair_real) - right_product(other_real, coupling)
    comm_imag = left_product(coupling, pair_imag) - right_product(other_imag, coupling)
    turned = jnp.transpose(eigenbasis)
    eigen_real = right_product(left_product(turned, -comm_imag), eigenbasis)
    eigen_imag = right_product(left_product(turned, comm_real), eigenbasis)
    damping = jnp.dot(occupation.astype(jnp.float32), decay_rates, precision=HIGHEST)[:, None, None]
    splitting = (energies[:, None] - energies[None, :])[None]
    denominator = damping * damping + splitting * splitting
    factor_real = -damping / denominator
    factor_imag = splitting / denominator
    solved_real = eigen_real * factor_real - eigen_imag * factor_imag
    solved_imag = eigen_real * factor_imag + eigen_imag * factor_real
    back_real = right_product(left_product(eigenbasis, solved_real), turned)
    back_imag = right_product(left_product(eigenbasis, solved_imag), turned)
    return jnp.stack([back_real, back_imag], axis=1)


def sweep_tier(lower_tier, upper_tier, local_table, peer_table, place_table, occupation,
               bath_coefficients, coupling, eigenbasis, energies, decay_rates):
    def one_device(device):
        row_major = device // N_MB
        row_minor = device % N_MB
        first_row = device * M_DEV
        within = jnp.arange(M_DEV, dtype=jnp.int32)
        raised_first = (((row_major + 1) % N_MA) * N_MB + row_minor) * M_DEV + within
        lowered_first = (((row_major + N_MA - 1) % N_MA) * N_MB + row_minor) * M_DEV + within
        nearby = lax.dynamic_slice_in_dim(local_table, first_row, M_DEV, 0)
        peer_ids = lax.dynamic_slice_in_dim(peer_table, first_row, M_DEV, 0)
        places = lax.dynamic_slice_in_dim(place_table, first_row, M_DEV, 0)
        counted = lax.dynamic_slice_in_dim(occupation, first_row, M_DEV, 0)
        remote = ((row_major * N_MB + peer_ids) * M_DEV + places).astype(jnp.int32)
        raised = jnp.concatenate([raised_first[:, None], remote[:, :2], first_row + nearby[:, 0, :]], axis=1)
        lowered = jnp.concatenate([lowered_first[:, None], remote[:, 2:], first_row + nearby[:, 1, :]], axis=1)
        up_sum = jnp.sum(upper_tier[raised], axis=1)
        lower_mats = lower_tier[lowered]
        weight_real = counted.astype(jnp.float32) * bath_coefficients[0][None, :]
        weight_imag = counted.astype(jnp.float32) * bath_coefficients[1][None, :]

        def weighted(weights, part_index):
            return jnp.einsum('mk,mkij->mij', weights, lower_mats[:, :, part_index], precision=HIGHEST)

        pair_real, pair_imag, other_real, other_imag = mix_terms(
            up_sum[:, 0], up_sum[:, 1], weighted(weight_real, 0), weighted(weight_real, 1),
            weighted(weight_imag, 0), weighted(weight_imag, 1))
        return settle(pair_real, pair_imag, other_real, other_imag, counted,
                      coupling, eigenbasis, energies, decay_rates)

    blocks = lax.map(one_device, jnp.arange(N_MA * N_MB, dtype=jnp.int32))
    return blocks.reshape(lower_tier.shape)


def reference(tier_four, tier_six, tier_seven, coupling, eigenbasis, energies, decay_rates, bath_coefficients,
              occupation_five, local_five, peers_five, places_five,
              occupation_six, local_six, peers_six, places_six):
    updated_five = sweep_tier(tier_four, tier_six, local_five, peers_five, places_five, occupation_five,
                              bath_coefficients, coupling, eigenbasis, energies, decay_rates)
    updated_six = sweep_tier(updated_five, tier_seven, local_six, peers_six, places_six, occupation_six,
                             bath_coefficients, coupling, eigenbasis, energies, decay_rates)
    return updated_five, updated_six
```

```python
import functools

import jax
import jax.numpy as jnp
from jax import lax
from jax.experimental import pallas as pl
from jax.experimental.pallas import tpu as pltpu
from jax.sharding import PartitionSpec as P

MESH = pl.DeviceIdType.MESH
F32, BF16 = jnp.float32, jnp.bfloat16
PARTS = 4
STRIDE = 11
LOWER_AT, COUNT_AT, TIER_AT = 11, 22, 64


def halves(x):
    high = x.astype(BF16)
    return high, (x - high.astype(F32)).astype(BF16)


def mxu(a, b):
    return jnp.dot(a, b, preferred_element_type=F32)


def dot3(a, b):
    return mxu(a[0], b[0]) + (mxu(a[0], b[1]) + mxu(a[1], b[0]))


def sweep_kernel(
    peers,
    rows,
    block,
    x4,
    x6,
    x7,
    tab_in,
    coupling,
    basis,
    energies,
    occ5,
    occ6,
    decay,
    bath,
    out5_hbm,
    out6_hbm,
    tab,
    s64,
    s7,
    s5,
    sums5,
    sums6,
    got5,
    got6,
    raised5,
    lowered5,
    raised6,
    lowered6,
    out5,
    out6,
    weights,
    stack,
    wide,
    left,
    split_sq,
    send_sems,
    recv_sems,
    own_sems,
    home_recv,
    home_own,
    out_sems,
):
    total = peers * block
    part = block // PARTS
    ma, me = lax.axis_index("ma"), lax.axis_index("mb")
    above = lax.rem(ma + 1, rows)
    below = lax.rem(ma + rows - 1, rows)

    def peer_of(j):
        return lax.rem(me + lax.rem(j * STRIDE, peers), peers)

    def each_peer(fn):
        def step(j, carry):
            fn(peer_of(j))
            return carry

        lax.fori_loop(1, peers, step, 0)

    def tile(d):
        return pl.ds(pl.multiple_of(d * 8, 8), 8)

    def remote(src, dst, k, recv, device):
        return pltpu.make_async_remote_copy(
            src_ref=src,
            dst_ref=dst,
            send_sem=send_sems.at[k],
            recv_sem=recv,
            device_id=device,
            device_id_type=MESH,
        )

    def arrived(ref, recv):
        remote(ref, ref, 0, recv, (ma, peer_of(1))).wait_recv()

    def sent(ref, k):
        remote(ref, ref, k, recv_sems.at[0], (ma, peer_of(1))).wait_send()

    barrier = pltpu.get_barrier_semaphore()
    each_peer(lambda d: pl.semaphore_signal(barrier, inc=1, device_id=(ma, d), device_id_type=MESH))
    pl.semaphore_signal(barrier, inc=1, device_id=(above, me), device_id_type=MESH)
    pl.semaphore_signal(barrier, inc=1, device_id=(below, me), device_id_type=MESH)

    mine = pl.ds(pl.multiple_of(me * block, block), block)
    own = [
        pltpu.make_async_copy(tab_in, tab.at[mine], own_sems.at[0]),
        pltpu.make_async_copy(x6.at[:, tile(me), :], s64.at[0, mine], own_sems.at[1]),
        pltpu.make_async_copy(x4.at[:, tile(me), :], s64.at[1, mine], own_sems.at[2]),
        pltpu.make_async_copy(x7.at[:, tile(me), :], s7.at[mine], own_sems.at[3]),
    ]
    for copy in own:
        copy.start()
    pl.semaphore_wait(barrier, peers + 1)

    def send_tables(d):
        remote(tab_in, tab.at[mine], 0, recv_sems.at[0], (ma, d)).start()

    def send_first(d):
        remote(x6.at[:, tile(d), :], s64.at[0, mine], 1, recv_sems.at[1], (ma, d)).start()
        remote(x4.at[:, tile(d), :], s64.at[1, mine], 1, recv_sems.at[1], (ma, d)).start()

    def send_seven(half):
        some = pl.ds(half * (block // 2), block // 2)
        there = pl.ds(pl.multiple_of(me * block + half * (block // 2), block // 2), block // 2)

        def fn(d):
            remote(x7.at[some, tile(d), :], s7.at[there], 2, recv_sems.at[2], (ma, d)).start()

        each_peer(fn)

    each_peer(send_tables)
    each_peer(send_first)
    ring = [
        remote(x6, raised5, 3, recv_sems.at[3], (below, me)),
        remote(x4, lowered5, 4, recv_sems.at[4], (above, me)),
        remote(x7, raised6, 5, recv_sems.at[5], (below, me)),
    ]
    for copy in ring:
        copy.start()
    send_seven(0)

    e = basis[...]
    c = coupling[...]
    turned = jnp.transpose(e)
    e2, c2, t2 = halves(e), halves(c), halves(turned)
    wide[0], wide[1] = e2
    wide[2], wide[3] = t2
    wide[4], wide[5] = halves(dot3(c2, e2))
    left[0, :, 0:128], left[1, :, 0:128] = halves(dot3(t2, c2))
    minus = halves(-turned)
    left[0, :, 128:256], left[1, :, 128:256] = minus
    across = jnp.broadcast_to(energies[...], (128, 128))
    split = jnp.transpose(across) - across
    split_sq[0] = split
    split_sq[1] = split * split

    own[0].wait()
    arrived(tab.at[pl.ds(0, total - block)], recv_sems.at[0])
    WR = 32

    def weigh(tier):
        def step(i, carry):
            at = pl.ds(pl.multiple_of(i * WR, WR), WR)
            t = tab[at, :]
            column = lax.broadcasted_iota(jnp.int32, (WR, total), 1)
            up = jnp.zeros((WR, total), F32)
            real = jnp.zeros((WR, total), F32)
            imag = jnp.zeros((WR, total), F32)
            for k in range(LOWER_AT):
                base = tier * TIER_AT + k
                hit = t[:, base : base + 1] == column
                up = up + jnp.where(hit, 1.0, 0.0)
                hit = t[:, base + LOWER_AT : base + LOWER_AT + 1] == column
                n = t[:, base + COUNT_AT : base + COUNT_AT + 1].astype(F32)
                real = real + jnp.where(hit, n * bath[0, k + 1], 0.0)
                imag = imag + jnp.where(hit, n * bath[1, k + 1], 0.0)
            rh, rl = halves(real)
            ih, il = halves(imag)
            u = up.astype(BF16)
            for spot, value in enumerate((u, u, rh, rh, rl)):
                weights[tier, 0, at, spot * total : (spot + 1) * total] = value
            for spot, value in enumerate((ih, ih, il)):
                weights[tier, 1, at, (spot + 2) * total : (spot + 3) * total] = value
            return carry

        lax.fori_loop(0, total // WR, step, 0)

    weigh(0)
    weigh(1)

    def prepare(flat, spots_high, spot_low):
        for s in range(8):
            high, low = halves(flat[pl.ds(s, total, stride=8), :])
            lanes = slice(128 * s, 128 * s + 128)
            for spot in spots_high:
                stack[spot * total : (spot + 1) * total, lanes] = high
            stack[spot_low * total : (spot_low + 1) * total, lanes] = low

    def combine(tier, sums):
        flat = sums.reshape(total * 16, 128)
        for pair in range(4):
            lanes = slice(256 * pair, 256 * pair + 256)
            a = mxu(weights[tier, 0], stack[:, lanes])
            b = mxu(weights[tier, 1, :, 2 * total :], stack[2 * total :, lanes])
            for t in range(2):
                s = 2 * pair + t
                flat[pl.ds(s, total, stride=16), :] = a[:, 128 * t : 128 * t + 128]
                flat[pl.ds(8 + s, total, stride=16), :] = b[:, 128 * t : 128 * t + 128]

    def send_home(tier, sums, got):
        def step(q, carry):
            here = pl.ds(q * part, part)
            at = pl.multiple_of(me * block + q * part, part)
            pltpu.make_async_copy(
                sums.at[pl.ds(at, part)], got.at[here, :, tile(me), :], home_own.at[tier, q]
            ).start()

            def fn(d):
                start = pl.multiple_of(d * block + q * part, part)
                remote(
                    sums.at[pl.ds(start, part)],
                    got.at[here, :, tile(me), :],
                    6 + tier,
                    home_recv.at[tier, q],
                    (ma, d),
                ).start()

            each_peer(fn)
            return carry

        lax.fori_loop(0, PARTS, step, 0)

    def got_home(tier, sums, got, q):
        here = pl.ds(q * part, part)
        at = pl.multiple_of(me * block + q * part, part)
        pltpu.make_async_copy(
            sums.at[pl.ds(at, part)], got.at[here, :, tile(me), :], home_own.at[tier, q]
        ).wait()
        arrived(got.at[here, :, pl.ds(0, 8 * (peers - 1)), :], home_recv.at[tier, q])

    def right(x, spot):
        return dot3(halves(x), (wide[spot], wide[spot + 1]))

    def settle(m, got, raised, lowered, occ, out):
        n = occ[m, 0].astype(F32)
        low = lowered[m]
        a = got[m, 0] + raised[m] + (n * bath[0, 0]) * low
        b = got[m, 1] + (n * bath[1, 0]) * low
        ar, ai, br, bi = a[0:128], a[128:256], b[0:128], b[128:256]
        first = right(jnp.concatenate([ar - bi, ai + br], axis=0), 0)
        second = right(jnp.concatenate([ar + bi, ai - br], axis=0), 4)
        both = jnp.concatenate(
            [
                jnp.concatenate([first[0:128], first[128:256]], axis=1),
                jnp.concatenate([second[0:128], second[128:256]], axis=1),
            ],
            axis=0,
        )
        comm = dot3((left[0], left[1]), halves(both))
        eigen_real, eigen_imag = -comm[:, 128:256], comm[:, 0:128]
        damping = jnp.float32(0.0)
        for k in range(12):
            damping = damping + occ[m, k].astype(F32) * decay[k]
        inverse = 1.0 / (damping * damping + split_sq[1])
        factor_real = -damping * inverse
        factor_imag = split_sq[0] * inverse
        solved = jnp.concatenate(
            [
                eigen_real * factor_real - eigen_imag * factor_imag,
                eigen_real * factor_imag + eigen_imag * factor_real,
            ],
            axis=0,
        )
        half = right(solved, 2)
        back = dot3(
            (wide[0], wide[1]),
            halves(jnp.concatenate([half[0:128], half[128:256]], axis=1)),
        )
        out[m, 0:128, :] = back[:, 0:128]
        out[m, 128:256, :] = back[:, 128:256]

    own[1].wait()
    own[2].wait()
    arrived(s64.at[:, pl.ds(0, total - block)], recv_sems.at[1])
    prepare(s64.at[0].reshape(total * 8, 128), (0,), 1)
    prepare(s64.at[1].reshape(total * 8, 128), (2, 4), 3)
    combine(0, sums5)
    send_home(0, sums5, got5)
    send_seven(1)
    arrived(raised5, recv_sems.at[3])
    arrived(lowered5, recv_sems.at[4])

    def tier_five(q, carry):
        got_home(0, sums5, got5, q)
        for r in range(part):
            settle(q * part + r, got5, raised5, lowered5, occ5, out5)
        here = pl.ds(q * part, part)
        there = pl.ds(pl.multiple_of(me * block + q * part, part), part)

        def fn(d):
            remote(out5.at[here, tile(d), :], s5.at[there], 8, recv_sems.at[6], (ma, d)).start()

        each_peer(fn)
        remote(out5.at[here], lowered6.at[here], 9, recv_sems.at[7], (above, me)).start()
        pltpu.make_async_copy(out5.at[here, tile(me), :], s5.at[there], own_sems.at[4]).start()
        pltpu.make_async_copy(out5.at[here], out5_hbm.at[here], out_sems.at[0]).start()
        return carry

    lax.fori_loop(0, PARTS, tier_five, 0)

    own[3].wait()
    arrived(s7.at[pl.ds(0, total - block)], recv_sems.at[2])
    prepare(s7.reshape(total * 8, 128), (0,), 1)
    pltpu.make_async_copy(s5.at[mine], s5.at[mine], own_sems.at[4]).wait()
    arrived(s5.at[pl.ds(0, total - block)], recv_sems.at[6])
    prepare(s5.reshape(total * 8, 128), (2, 4), 3)
    combine(1, sums6)
    send_home(1, sums6, got6)
    arrived(raised6, recv_sems.at[5])
    arrived(lowered6, recv_sems.at[7])

    def tier_six(q, carry):
        got_home(1, sums6, got6, q)
        for r in range(part):
            settle(q * part + r, got6, raised6, lowered6, occ6, out6)
        here = pl.ds(q * part, part)
        pltpu.make_async_copy(out6.at[here], out6_hbm.at[here], out_sems.at[1]).start()
        return carry

    lax.fori_loop(0, PARTS, tier_six, 0)

    most = pl.ds(0, total - block)
    sent(tab.at[most], 0)
    sent(s64.at[:, most], 1)
    sent(s7.at[most], 2)
    for k, copy in enumerate(ring):
        copy.wait_send()
    sent(sums5.at[most], 6)
    sent(sums6.at[most], 7)
    sent(s5.at[most], 8)
    sent(lowered6, 9)
    pltpu.make_async_copy(out5, out5_hbm, out_sems.at[0]).wait()
    pltpu.make_async_copy(out6, out6_hbm, out_sems.at[1]).wait()


def table_of(local, peers, places, occupation, block):
    base = lax.axis_index("mb").astype(jnp.int32) * block
    remote = peers * block + places
    near = local + base
    return jnp.concatenate(
        [remote[:, :2], near[:, 0], remote[:, 2:], near[:, 1], occupation[:, 1:]], axis=1
    )


def body(
    rows,
    peers,
    tier_four,
    tier_six,
    tier_seven,
    coupling,
    eigenbasis,
    energies,
    decay_rates,
    bath_coefficients,
    occupation_five,
    local_five,
    peers_five,
    places_five,
    occupation_six,
    local_six,
    peers_six,
    places_six,
):
    block = tier_four.shape[0]
    total = peers * block
    shape = tier_four.shape
    table = jnp.concatenate(
        [
            jnp.pad(table_of(local_five, peers_five, places_five, occupation_five, block), ((0, 0), (0, 31))),
            jnp.pad(table_of(local_six, peers_six, places_six, occupation_six, block), ((0, 0), (0, 31))),
        ],
        axis=1,
    )
    flat = (block, 256, 128)
    any_space = pl.BlockSpec(memory_space=pl.ANY)
    vmem = pl.BlockSpec(memory_space=pltpu.VMEM)
    smem = pl.BlockSpec(memory_space=pltpu.SMEM)
    out = jax.ShapeDtypeStruct(flat, F32)
    store = pltpu.VMEM((total, 8, 128), F32)
    sums = pltpu.VMEM((total, 2, 8, 128), F32)
    got = pltpu.VMEM((block, 2, 256, 128), F32)
    whole = pltpu.VMEM(flat, F32)
    dma = pltpu.SemaphoreType.DMA
    five, six = pl.pallas_call(
        functools.partial(sweep_kernel, peers, rows, block),
        out_shape=(out, out),
        in_specs=[any_space] * 3 + [vmem] * 4 + [smem] * 4,
        out_specs=(any_space, any_space),
        scratch_shapes=[
            pltpu.VMEM((total, 128), jnp.int32),
            pltpu.VMEM((2, total, 8, 128), F32),
            store,
            store,
            sums,
            sums,
            got,
            got,
            whole,
            whole,
            whole,
            whole,
            whole,
            whole,
            pltpu.VMEM((2, 2, total, 5 * total), BF16),
            pltpu.VMEM((5 * total, 1024), BF16),
            pltpu.VMEM((6, 128, 128), BF16),
            pltpu.VMEM((2, 128, 256), BF16),
            pltpu.VMEM((2, 128, 128), F32),
            dma((10,)),
            dma((8,)),
            dma((5,)),
            dma((2, PARTS)),
            dma((2, PARTS)),
            dma((2,)),
        ],
        compiler_params=pltpu.CompilerParams(
            collective_id=0, has_side_effects=True, vmem_limit_bytes=60 * 1024 * 1024
        ),
        name="sweep",
    )(
        tier_four.reshape(flat),
        tier_six.reshape(flat),
        tier_seven.reshape(flat),
        table,
        coupling,
        eigenbasis,
        energies.reshape(1, -1),
        occupation_five,
        occupation_six,
        decay_rates,
        bath_coefficients,
    )
    return five.reshape(shape), six.reshape(shape)


def solution(mesh):
    rows, peers = mesh.shape["ma"], mesh.shape["mb"]
    whole = P(("ma", "mb"), None, None, None)
    wide = P(("ma", "mb"), None)
    tables = (wide, P(("ma", "mb"), None, None), wide, wide)
    in_specs = (whole,) * 3 + (P(),) * 5 + tables + tables
    return jax.shard_map(
        functools.partial(body, rows, peers),
        mesh=mesh,
        in_specs=in_specs,
        out_specs=(whole, whole),
        check_vma=False,
    )
```

```python
import functools

import jax
import jax.numpy as jnp
from jax import lax
from jax.experimental import pallas as pl
from jax.experimental.pallas import tpu as pltpu
from jax.sharding import PartitionSpec as P

MESH = pl.DeviceIdType.MESH
F32, BF16 = jnp.float32, jnp.bfloat16
PARTS = 4
STRIDE = 11
LOWER_AT, REAL_AT, IMAG_AT, TIER_AT = 11, 22, 33, 64


def halves(x):
    high = x.astype(BF16)
    return high, (x - high.astype(F32)).astype(BF16)


def mxu(a, b):
    return jnp.dot(a, b, preferred_element_type=F32)


def dot3(a, b):
    return mxu(a[0], b[0]) + (mxu(a[0], b[1]) + mxu(a[1], b[0]))


def sweep_kernel(
    peers,
    rows,
    block,
    x4,
    x6,
    x7,
    *refs,
):
    small, refs = refs[:13], refs[13:]
    out5, out6, *refs = refs
    local, refs = refs[:13], refs[13:]
    run(peers, rows, block, x4, x6, x7, small, local, out5, out6, *refs)


def run(
    peers,
    rows,
    block,
    x4,
    x6,
    x7,
    small,
    local,
    out5,
    out6,
    tab_in,
    tab,
    s64,
    s7,
    s5,
    sums5,
    sums6,
    got5,
    got6,
    raised5,
    lowered5,
    raised6,
    lowered6,
    weights,
    stack,
    wide,
    left,
    split_sq,
    rates,
    send_sems,
    recv_sems,
    own_sems,
    home_recv,
    home_own,
    small_sems,
):
    total = peers * block
    part = block // PARTS
    ma, me = lax.axis_index("ma"), lax.axis_index("mb")
    above = lax.rem(ma + 1, rows)
    below = lax.rem(ma + rows - 1, rows)

    def peer_of(j):
        return lax.rem(me + lax.rem(j * STRIDE, peers), peers)

    def each_peer(fn):
        def step(j, carry):
            fn(peer_of(j))
            return carry

        lax.fori_loop(1, peers, step, 0)

    def tile(d):
        return pl.ds(pl.multiple_of(d * 8, 8), 8)

    def remote(src, dst, k, recv, device):
        return pltpu.make_async_remote_copy(
            src_ref=src,
            dst_ref=dst,
            send_sem=send_sems.at[k],
            recv_sem=recv,
            device_id=device,
            device_id_type=MESH,
        )

    def arrived(ref, recv):
        remote(ref, ref, 0, recv, (ma, peer_of(1))).wait_recv()

    def sent(ref, k):
        remote(ref, ref, k, recv_sems.at[0], (ma, peer_of(1))).wait_send()

    fetch = [
        pltpu.make_async_copy(a, b, small_sems.at[i]) for i, (a, b) in enumerate(zip(small, local))
    ]
    for copy in fetch:
        copy.start()
    coupling, basis, energies, decay, bath, *tables = local

    barrier = pltpu.get_barrier_semaphore()
    each_peer(lambda d: pl.semaphore_signal(barrier, inc=1, device_id=(ma, d), device_id_type=MESH))
    pl.semaphore_signal(barrier, inc=1, device_id=(above, me), device_id_type=MESH)
    pl.semaphore_signal(barrier, inc=1, device_id=(below, me), device_id_type=MESH)

    mine = pl.ds(pl.multiple_of(me * block, block), block)
    own = [
        pltpu.make_async_copy(tab_in, tab.at[mine], own_sems.at[0]),
        pltpu.make_async_copy(x6.at[:, tile(me), :], s64.at[0, mine], own_sems.at[1]),
        pltpu.make_async_copy(x4.at[:, tile(me), :], s64.at[1, mine], own_sems.at[2]),
        pltpu.make_async_copy(x7.at[:, tile(me), :], s7.at[mine], own_sems.at[3]),
    ]
    for copy in own[1:]:
        copy.start()
    for copy in fetch:
        copy.wait()
    lane = lax.broadcasted_iota(jnp.int32, (block, 128), 1)
    on_diagonal = lax.broadcasted_iota(jnp.int32, (block, block), 0) == lax.broadcasted_iota(
        jnp.int32, (block, block), 1
    )
    entries = jnp.zeros((block, 128), F32)

    def put(entries, at, column):
        return jnp.where(lane == at, jnp.broadcast_to(column, (block, 128)), entries)

    for tier in range(2):
        occupation, near, peer_ids, places = tables[4 * tier : 4 * tier + 4]
        base = tier * TIER_AT
        wanted = (peer_ids[...] * block + places[...]).astype(F32)
        for k in range(4):
            row = jnp.broadcast_to(wanted[k : k + 1, :], (block, block))
            column = jnp.sum(jnp.where(on_diagonal, row, 0.0), axis=1, keepdims=True)
            entries = put(entries, base + (k if k < 2 else LOWER_AT + k - 2), column)
        inside = (near[...] + me * block).astype(F32)
        up, low = inside[:, 0, :], inside[:, 1, :]
        for k in range(9):
            entries = put(entries, base + 2 + k, up[:, k : k + 1])
            entries = put(entries, base + LOWER_AT + 2 + k, low[:, k : k + 1])
        counted = occupation[...].astype(F32)
        real = counted * bath[0:1, :]
        imag = counted * bath[1:2, :]
        for k in range(11):
            entries = put(entries, base + REAL_AT + k, real[:, k + 1 : k + 2])
            entries = put(entries, base + IMAG_AT + k, imag[:, k + 1 : k + 2])
        damp = jnp.sum(counted * decay[...], axis=1, keepdims=True)
        for spot, column in enumerate((real[:, 0:1], imag[:, 0:1], damp)):
            rates[tier, spot] = jnp.broadcast_to(column, (block, 128))
    tab_in[...] = entries
    own[0].start()
    pl.semaphore_wait(barrier, peers + 1)

    def send_tables(d):
        remote(tab_in, tab.at[mine], 0, recv_sems.at[0], (ma, d)).start()

    def send_first(d):
        remote(x6.at[:, tile(d), :], s64.at[0, mine], 1, recv_sems.at[1], (ma, d)).start()
        remote(x4.at[:, tile(d), :], s64.at[1, mine], 1, recv_sems.at[1], (ma, d)).start()

    def send_seven(half):
        some = pl.ds(half * (block // 2), block // 2)
        there = pl.ds(pl.multiple_of(me * block + half * (block // 2), block // 2), block // 2)

        def fn(d):
            remote(x7.at[some, tile(d), :], s7.at[there], 2, recv_sems.at[2], (ma, d)).start()

        each_peer(fn)

    each_peer(send_tables)
    each_peer(send_first)
    ring = [
        remote(x6, raised5, 3, recv_sems.at[3], (below, me)),
        remote(x4, lowered5, 4, recv_sems.at[4], (above, me)),
        remote(x7, raised6, 5, recv_sems.at[5], (below, me)),
    ]
    for copy in ring:
        copy.start()
    send_seven(0)

    e = basis[...]
    c = coupling[...]
    turned = jnp.transpose(e)
    e2, c2, t2 = halves(e), halves(c), halves(turned)
    wide[0], wide[1] = e2
    wide[2], wide[3] = t2
    wide[4], wide[5] = halves(dot3(c2, e2))
    left[0, :, 0:128], left[1, :, 0:128] = halves(dot3(t2, c2))
    minus = halves(-turned)
    left[0, :, 128:256], left[1, :, 128:256] = minus
    across = jnp.broadcast_to(energies[...], (128, 128))
    split = jnp.transpose(across) - across
    split_sq[0] = split
    split_sq[1] = split * split

    own[0].wait()
    arrived(tab.at[pl.ds(0, total - block)], recv_sems.at[0])
    WR = 32

    def weigh(tier):
        def step(i, carry):
            at = pl.ds(pl.multiple_of(i * WR, WR), WR)
            t = tab[at, :]
            column = lax.broadcasted_iota(jnp.int32, (WR, total), 1).astype(F32)
            up = jnp.zeros((WR, total), F32)
            real = jnp.zeros((WR, total), F32)
            imag = jnp.zeros((WR, total), F32)
            for k in range(LOWER_AT):
                base = tier * TIER_AT + k
                hit = t[:, base : base + 1] == column
                up = up + jnp.where(hit, 1.0, 0.0)
                hit = t[:, base + LOWER_AT : base + LOWER_AT + 1] == column
                real = real + jnp.where(hit, t[:, base + REAL_AT : base + REAL_AT + 1], 0.0)
                imag = imag + jnp.where(hit, t[:, base + IMAG_AT : base + IMAG_AT + 1], 0.0)
            rh, rl = halves(real)
            ih, il = halves(imag)
            u = up.astype(BF16)
            for spot, value in enumerate((u, u, rh, rh, rl)):
                weights[tier, 0, at, spot * total : (spot + 1) * total] = value
            for spot, value in enumerate((ih, ih, il)):
                weights[tier, 1, at, (spot + 2) * total : (spot + 3) * total] = value
            return carry

        lax.fori_loop(0, total // WR, step, 0)

    weigh(0)
    weigh(1)

    def prepare(flat, spots_high, spot_low):
        for s in range(8):
            high, low = halves(flat[pl.ds(s, total, stride=8), :])
            lanes = slice(128 * s, 128 * s + 128)
            for spot in spots_high:
                stack[spot * total : (spot + 1) * total, lanes] = high
            stack[spot_low * total : (spot_low + 1) * total, lanes] = low

    def combine(tier, kind, sums):
        flat = sums.at[kind].reshape(total * 8, 128)
        first = 2 * kind * total
        for pair in range(4):
            lanes = slice(256 * pair, 256 * pair + 256)
            a = mxu(weights[tier, kind, :, first:], stack[first:, lanes])
            for t in range(2):
                flat[pl.ds(2 * pair + t, total, stride=8), :] = a[:, 128 * t : 128 * t + 128]

    def send_home(tier, kind, sums, got, q, size):
        here = pl.ds(pl.multiple_of(q * size, size), size)
        slot = home_own.at[tier, q] if kind == 0 else home_own.at[tier, PARTS]
        recv = home_recv.at[tier, q] if kind == 0 else home_recv.at[tier, PARTS]
        at = pl.multiple_of(me * block + q * size, size)
        pltpu.make_async_copy(
            sums.at[kind, pl.ds(at, size)], got.at[kind, here, tile(me), :], slot
        ).start()

        def fn(d):
            start = pl.multiple_of(d * block + q * size, size)
            remote(
                sums.at[kind, pl.ds(start, size)],
                got.at[kind, here, tile(me), :],
                6 + tier,
                recv,
                (ma, d),
            ).start()

        each_peer(fn)

    def send_parts(tier, sums, got):
        def step(q, carry):
            send_home(tier, 0, sums, got, q, part)
            return carry

        lax.fori_loop(0, PARTS, step, 0)

    def got_home(tier, kind, got, q, size):
        here = pl.ds(pl.multiple_of(q * size, size), size)
        slot = home_own.at[tier, q] if kind == 0 else home_own.at[tier, PARTS]
        recv = home_recv.at[tier, q] if kind == 0 else home_recv.at[tier, PARTS]
        ref = got.at[kind, here, tile(me), :]
        pltpu.make_async_copy(ref, ref, slot).wait()
        arrived(got.at[kind, here, pl.ds(0, 8 * (peers - 1)), :], recv)

    def right(x, spot):
        return dot3(halves(x), (wide[spot], wide[spot + 1]))

    def settle(tier, m, got, raised, lowered, out):
        low = lowered[m]
        real = rates[tier, 0, pl.ds(m, 1), :]
        imag = rates[tier, 1, pl.ds(m, 1), :]
        damping = jnp.broadcast_to(rates[tier, 2, pl.ds(m, 1), :], (128, 128))
        a = got[0, m] + raised[m] + real * low
        b = got[1, m] + imag * low
        ar, ai, br, bi = a[0:128], a[128:256], b[0:128], b[128:256]
        first = right(jnp.concatenate([ar - bi, ai + br], axis=0), 0)
        second = right(jnp.concatenate([ar + bi, ai - br], axis=0), 4)
        both = jnp.concatenate(
            [
                jnp.concatenate([first[0:128], first[128:256]], axis=1),
                jnp.concatenate([second[0:128], second[128:256]], axis=1),
            ],
            axis=0,
        )
        comm = dot3((left[0], left[1]), halves(both))
        eigen_real, eigen_imag = -comm[:, 128:256], comm[:, 0:128]
        inverse = 1.0 / (damping * damping + split_sq[1])
        factor_real = -damping * inverse
        factor_imag = split_sq[0] * inverse
        solved = jnp.concatenate(
            [
                eigen_real * factor_real - eigen_imag * factor_imag,
                eigen_real * factor_imag + eigen_imag * factor_real,
            ],
            axis=0,
        )
        half = right(solved, 2)
        back = dot3(
            (wide[0], wide[1]),
            halves(jnp.concatenate([half[0:128], half[128:256]], axis=1)),
        )
        out[m, 0:128, :] = back[:, 0:128]
        out[m, 128:256, :] = back[:, 128:256]

    own[1].wait()
    own[2].wait()
    arrived(s64.at[:, pl.ds(0, total - block)], recv_sems.at[1])
    prepare(s64.at[0].reshape(total * 8, 128), (0,), 1)
    prepare(s64.at[1].reshape(total * 8, 128), (2, 4), 3)
    combine(0, 1, sums5)
    send_home(0, 1, sums5, got5, 0, block)
    combine(0, 0, sums5)
    send_parts(0, sums5, got5)
    arrived(raised5, recv_sems.at[3])
    arrived(lowered5, recv_sems.at[4])
    got_home(0, 1, got5, 0, block)

    def tier_five(q, carry):
        got_home(0, 0, got5, q, part)
        for r in range(part):
            settle(0, q * part + r, got5, raised5, lowered5, out5)
        here = pl.ds(q * part, part)
        there = pl.ds(pl.multiple_of(me * block + q * part, part), part)

        def fn(d):
            remote(out5.at[here, tile(d), :], s5.at[there], 8, recv_sems.at[6], (ma, d)).start()

        each_peer(fn)
        remote(out5.at[here], lowered6.at[here], 9, recv_sems.at[7], (above, me)).start()
        pltpu.make_async_copy(out5.at[here, tile(me), :], s5.at[there], own_sems.at[4]).start()
        return carry

    lax.fori_loop(0, PARTS, tier_five, 0)
    send_seven(1)

    pltpu.make_async_copy(s5.at[mine], s5.at[mine], own_sems.at[4]).wait()
    arrived(s5.at[pl.ds(0, total - block)], recv_sems.at[6])
    prepare(s5.reshape(total * 8, 128), (2, 4), 3)
    combine(1, 1, sums6)
    send_home(1, 1, sums6, got6, 0, block)
    own[3].wait()
    arrived(s7.at[pl.ds(0, total - block)], recv_sems.at[2])
    prepare(s7.reshape(total * 8, 128), (0,), 1)
    combine(1, 0, sums6)
    send_parts(1, sums6, got6)
    arrived(raised6, recv_sems.at[5])
    arrived(lowered6, recv_sems.at[7])
    got_home(1, 1, got6, 0, block)

    def tier_six(q, carry):
        got_home(1, 0, got6, q, part)
        for r in range(part):
            settle(1, q * part + r, got6, raised6, lowered6, out6)
        return carry

    lax.fori_loop(0, PARTS, tier_six, 0)

    most = pl.ds(0, total - block)
    sent(tab.at[most], 0)
    sent(s64.at[:, most], 1)
    sent(s7.at[most], 2)
    for copy in ring:
        copy.wait_send()
    sent(sums5.at[:, most], 6)
    sent(sums6.at[:, most], 7)
    sent(s5.at[most], 8)
    sent(lowered6, 9)


def body(
    rows,
    peers,
    tier_four,
    tier_six,
    tier_seven,
    coupling,
    eigenbasis,
    energies,
    decay_rates,
    bath_coefficients,
    occupation_five,
    local_five,
    peers_five,
    places_five,
    occupation_six,
    local_six,
    peers_six,
    places_six,
):
    block = tier_four.shape[0]
    total = peers * block
    shape = tier_four.shape
    flat = (block, 256, 128)
    hbm = pl.BlockSpec(memory_space=pltpu.HBM)
    small = (
        coupling,
        eigenbasis,
        energies.reshape(1, -1),
        decay_rates.reshape(1, -1),
        bath_coefficients,
        occupation_five,
        local_five,
        peers_five.T,
        places_five.T,
        occupation_six,
        local_six,
        peers_six.T,
        places_six.T,
    )
    store = pltpu.VMEM((total, 8, 128), F32)
    sums = pltpu.VMEM((2, total, 8, 128), F32)
    got = pltpu.VMEM((2, block, 256, 128), F32)
    whole = pltpu.VMEM(flat, F32)
    dma = pltpu.SemaphoreType.DMA
    five, six = pl.pallas_call(
        functools.partial(sweep_kernel, peers, rows, block),
        out_shape=(pltpu.VMEM(flat, F32), pltpu.VMEM(flat, F32)),
        in_specs=[hbm] * 16,
        scratch_shapes=[pltpu.VMEM(a.shape, a.dtype) for a in small]
        + [
            pltpu.VMEM((block, 128), F32),
            pltpu.VMEM((total, 128), F32),
            pltpu.VMEM((2, total, 8, 128), F32),
            store,
            store,
            sums,
            sums,
            got,
            got,
            whole,
            whole,
            whole,
            whole,
            pltpu.VMEM((2, 2, total, 5 * total), BF16),
            pltpu.VMEM((5 * total, 1024), BF16),
            pltpu.VMEM((6, 128, 128), BF16),
            pltpu.VMEM((2, 128, 256), BF16),
            pltpu.VMEM((2, 128, 128), F32),
            pltpu.VMEM((2, 3, block, 128), F32),
            dma((10,)),
            dma((8,)),
            dma((5,)),
            dma((2, PARTS + 1)),
            dma((2, PARTS + 1)),
            dma((13,)),
        ],
        compiler_params=pltpu.CompilerParams(
            collective_id=0, has_side_effects=True, vmem_limit_bytes=64946176
        ),
        name="sweep",
    )(
        tier_four.reshape(flat),
        tier_six.reshape(flat),
        tier_seven.reshape(flat),
        *small,
    )
    return five.reshape(shape), six.reshape(shape)


def solution(mesh):
    rows, peers = mesh.shape["ma"], mesh.shape["mb"]
    whole = P(("ma", "mb"), None, None, None)
    wide = P(("ma", "mb"), None)
    tables = (wide, P(("ma", "mb"), None, None), wide, wide)
    in_specs = (whole,) * 3 + (P(),) * 5 + tables + tables
    return jax.shard_map(
        functools.partial(body, rows, peers),
        mesh=mesh,
        in_specs=in_specs,
        out_specs=(whole, whole),
        check_vma=False,
    )
```

```python
import functools

import jax
import jax.numpy as jnp
from jax import lax
from jax.experimental import pallas as pl
from jax.experimental.pallas import tpu as pltpu
from jax.sharding import PartitionSpec as P

MESH = pl.DeviceIdType.MESH
F32, BF16 = jnp.float32, jnp.bfloat16
PARTS = 4
STRIDE = 11
LOWER_AT, REAL_AT, IMAG_AT, DAMP_AT, TIER_AT = 11, 22, 34, 46, 64
N_SMALL = 13


def halves(x):
    high = x.astype(BF16)
    return high, (x - high.astype(F32)).astype(BF16)


def mxu(a, b):
    return jnp.dot(a, b, preferred_element_type=F32)


def dot3(a, b):
    return mxu(a[0], b[0]) + (mxu(a[0], b[1]) + mxu(a[1], b[0]))


def beside(x):
    return jnp.concatenate([x[0:128], x[128:256]], axis=1)


EVEN, ODD = pl.ds(0, 128, stride=2), pl.ds(1, 128, stride=2)


def sweep_kernel(peers, rows, block, x4, x6, x7, *refs):
    small, refs = refs[:N_SMALL], refs[N_SMALL:]
    out5, out6, *refs = refs
    local, refs = refs[:N_SMALL], refs[N_SMALL:]
    run(peers, rows, block, (x4, x6, x7), small, local, out5, out6, *refs)


def run(
    peers,
    rows,
    block,
    tiers,
    small,
    local,
    out5,
    out6,
    tab_in,
    tab,
    tab_above,
    held,
    d6,
    ds4,
    d7,
    p5,
    sd6,
    sds4,
    sd7,
    sp5,
    m4,
    m4y,
    d6y,
    d7y,
    y5,
    got5,
    got6,
    sums5,
    sums6,
    drive,
    solved,
    turned_by,
    z6,
    above_weights,
    damp_all,
    weights,
    stack,
    wide,
    both_right,
    split_sq,
    rates,
    send_sems,
    recv_sems,
    part_sems,
    own_sems,
    own_parts,
    small_sems,
):
    total = peers * block
    part = block // PARTS
    rows_part = part * peers
    ma, me = lax.axis_index("ma"), lax.axis_index("mb")
    above = lax.rem(ma + 1, rows)
    below = lax.rem(ma + rows - 1, rows)

    def each_peer(fn):
        def step(j, carry):
            fn(lax.rem(me + lax.rem(j * STRIDE, peers), peers))
            return carry

        lax.fori_loop(1, peers, step, 0)

    def tile(d):
        return pl.ds(pl.multiple_of(d * 8, 8), 8)

    def chunk(q):
        return pl.ds(pl.multiple_of(q * part, part), part)

    others = pl.ds(0, peers - 1)

    def remote(src, dst, k, recv, device):
        return pltpu.make_async_remote_copy(
            src_ref=src,
            dst_ref=dst,
            send_sem=send_sems.at[k],
            recv_sem=recv,
            device_id=device,
            device_id_type=MESH,
        )

    def arrived(ref, recv):
        remote(ref, ref, 0, recv, (above, me)).wait_recv()

    def sent(ref, k):
        remote(ref, ref, k, recv_sems.at[0], (above, me)).wait_send()

    def here(ref, sem):
        pltpu.make_async_copy(ref, ref, sem).wait()

    def flat(ref):
        return ref.reshape(total * 8, 128)

    fetch = [
        pltpu.make_async_copy(a, b, small_sems.at[i]) for i, (a, b) in enumerate(zip(small, local))
    ]
    for copy in fetch:
        copy.start()
    load = [pltpu.make_async_copy(a, held.at[i], own_sems.at[1 + i]) for i, a in enumerate(tiers)]
    for i in (1, 0, 2):
        load[i].start()
    coupling, basis, energies, decay, bath, *tables = local

    barrier = pltpu.get_barrier_semaphore()
    each_peer(lambda d: pl.semaphore_signal(barrier, inc=1, device_id=(ma, d), device_id_type=MESH))
    pl.semaphore_signal(barrier, inc=1, device_id=(above, me), device_id_type=MESH)
    pl.semaphore_signal(barrier, inc=1, device_id=(below, me), device_id_type=MESH)

    for copy in fetch:
        copy.wait()
    lane = lax.broadcasted_iota(jnp.int32, (block, 128), 1)
    on_diagonal = lax.broadcasted_iota(jnp.int32, (block, block), 0) == lax.broadcasted_iota(
        jnp.int32, (block, block), 1
    )
    entries = jnp.zeros((block, 128), F32)

    def put(entries, at, column):
        return jnp.where(lane == at, jnp.broadcast_to(column, (block, 128)), entries)

    for tier in range(2):
        occupation, near, peer_ids, places = tables[4 * tier : 4 * tier + 4]
        base = tier * TIER_AT
        wanted = (places[...] * peers + peer_ids[...]).astype(F32)
        for k in range(4):
            row = jnp.broadcast_to(wanted[k : k + 1, :], (block, block))
            column = jnp.sum(jnp.where(on_diagonal, row, 0.0), axis=1, keepdims=True)
            entries = put(entries, base + (k if k < 2 else LOWER_AT + k - 2), column)
        inside = (near[...] * peers + me).astype(F32)
        up, low = inside[:, 0, :], inside[:, 1, :]
        for k in range(9):
            entries = put(entries, base + 2 + k, up[:, k : k + 1])
            entries = put(entries, base + LOWER_AT + 2 + k, low[:, k : k + 1])
        counted = occupation[...].astype(F32)
        real = counted * bath[0:1, :]
        imag = counted * bath[1:2, :]
        for k in range(12):
            entries = put(entries, base + REAL_AT + k, real[:, k : k + 1])
            entries = put(entries, base + IMAG_AT + k, imag[:, k : k + 1])
        damp = jnp.sum(counted * decay[...], axis=1, keepdims=True)
        entries = put(entries, base + DAMP_AT, damp)
    for spot, column in enumerate((real[:, 0:1], imag[:, 0:1], damp)):
        rates[spot] = jnp.broadcast_to(column, (block, 128))
    tab_in[...] = entries
    mine = pl.ds(pl.multiple_of(me * block, block), block)
    own_tab = pltpu.make_async_copy(tab_in, tab.at[mine], own_sems.at[0])
    own_tab.start()

    e = basis[...]
    turned = jnp.transpose(e)
    e2, c2, t2 = halves(e), halves(coupling[...]), halves(turned)
    wide[0], wide[1] = e2
    wide[2], wide[3] = t2
    ce = halves(dot3(c2, e2))
    wide[4], wide[5] = halves(dot3(t2, ce))
    wide[6], wide[7] = halves(dot3(t2, c2))
    for i in range(2):
        both_right[i, :, 0:128] = e2[i]
        both_right[i, :, 128:256] = ce[i]
    across = jnp.broadcast_to(energies[...], (128, 128))
    split = jnp.transpose(across) - across
    split_sq[0] = split
    split_sq[1] = split * split

    def const(k):
        return wide[2 * k], wide[2 * k + 1]

    basis_at, turned_at, coupled_at, from_left_at = 0, 1, 2, 3

    def products(x):
        t = dot3(halves(x), (both_right[0], both_right[1]))
        left = dot3(const(from_left_at), halves(beside(t[:, 0:128])))
        right = dot3(const(turned_at), halves(beside(t[:, 128:256])))
        return left, right

    def put_commutator(ref, p, q):
        c = p - q
        ref[EVEN, :] = -c[:, 128:256]
        ref[ODD, :] = c[:, 0:128]

    def commutators(which, out, first, count):
        def step(m, carry):
            p, q = products(held[which, m])
            put_commutator(out.at[m], p, q)
            return carry

        lax.fori_loop(first, first + count, step, 0)

    def scatter(src, dst, k, recv, some):
        def fn(d):
            remote(src.at[some, tile(d), :], dst.at[some, me], k, recv, (ma, d)).start()

        each_peer(fn)

    half = block // 2
    load[1].wait()
    commutators(1, d6, 0, half)
    pl.semaphore_wait(barrier, peers + 1)
    each_peer(lambda d: remote(tab_in, tab.at[mine], 0, recv_sems.at[0], (ma, d)).start())
    scatter(d6, sd6, 1, recv_sems.at[1], pl.ds(0, half))
    commutators(1, d6, half, half)
    scatter(d6, sd6, 1, recv_sems.at[1], pl.ds(half, half))
    everything = pl.ds(0, block)
    pltpu.make_async_copy(d6.at[:, tile(me), :], sd6.at[:, me], own_sems.at[4]).start()

    load[0].wait()

    def tier_four(q, carry):
        for r in range(part):
            m = q * part + r
            p, s = products(held[0, m])
            put_commutator(ds4.at[0, m], p, s)
            both = p + s
            ds4[1, m, EVEN, :] = both[:, 0:128]
            ds4[1, m, ODD, :] = both[:, 128:256]

        def fn(d):
            remote(
                ds4.at[:, chunk(q), tile(d), :],
                sds4.at[:, chunk(q), me],
                2,
                part_sems.at[0, q],
                (ma, d),
            ).start()

        each_peer(fn)
        pltpu.make_async_copy(
            ds4.at[:, chunk(q), tile(me), :], sds4.at[:, chunk(q), me], own_parts.at[0, q]
        ).start()
        return carry

    lax.fori_loop(0, PARTS, tier_four, 0)

    load[2].wait()
    commutators(2, d7, 0, block)
    scatter(d7, sd7, 3, recv_sems.at[2], everything)
    pltpu.make_async_copy(d7.at[:, tile(me), :], sd7.at[:, me], own_sems.at[5]).start()

    own_tab.wait()
    arrived(tab.at[pl.ds(0, total - block)], recv_sems.at[0])
    remote(tab, tab_above, 4, recv_sems.at[3], (below, me)).start()
    here(sd6.at[:, me], own_sems.at[4])
    arrived(sd6.at[:, others], recv_sems.at[1])
    remote(sd6, d6y, 5, recv_sems.at[4], (below, me)).start()
    remote(d7, d7y, 6, recv_sems.at[5], (below, me)).start()

    def weigh(tier):
        base = tier * TIER_AT

        def step(i, carry):
            at = pl.ds(pl.multiple_of(i * peers, peers), peers)
            t = tab[pl.ds(i, peers, stride=block), :]
            column = lax.broadcasted_iota(jnp.int32, (peers, total), 1).astype(F32)
            up = jnp.zeros((peers, total), F32)
            real = jnp.zeros((peers, total), F32)
            imag = jnp.zeros((peers, total), F32)
            for k in range(11):
                hit = t[:, base + k : base + k + 1] == column
                up = up + jnp.where(hit, 1.0, 0.0)
                hit = t[:, base + LOWER_AT + k : base + LOWER_AT + k + 1] == column
                wr = t[:, base + REAL_AT + k + 1 : base + REAL_AT + k + 2]
                wi = t[:, base + IMAG_AT + k + 1 : base + IMAG_AT + k + 2]
                real = real + jnp.where(hit, wr, 0.0)
                imag = imag - jnp.where(hit, wi, 0.0)
            rh, rl = halves(real)
            ih, il = halves(imag)
            u = up.astype(BF16)
            for spot, value in enumerate((u, u, rh, rh, rl, ih, ih, il)):
                weights[tier, at, spot * total : (spot + 1) * total] = value
            if tier == 0:
                damp_all[at, :] = jnp.broadcast_to(t[:, DAMP_AT : DAMP_AT + 1], (peers, 128))
            return carry

        lax.fori_loop(0, block, step, 0)

    weigh(0)
    arrived(tab_above, recv_sems.at[3])

    def next_row(i, carry):
        at = pl.ds(pl.multiple_of(i * peers, peers), peers)
        t = tab_above[pl.ds(i, peers, stride=block), :]
        above_weights[0, at, :] = jnp.broadcast_to(t[:, REAL_AT : REAL_AT + 1], (peers, 128))
        above_weights[1, at, :] = jnp.broadcast_to(t[:, IMAG_AT : IMAG_AT + 1], (peers, 128))
        return carry

    lax.fori_loop(0, block, next_row, 0)

    def store_halves(at, lanes, value, spots_high, spot_low):
        high, low = halves(value)
        for spot in spots_high:
            stack[pl.ds(at + spot * total, value.shape[0]), lanes] = high
        stack[pl.ds(at + spot_low * total, value.shape[0]), lanes] = low

    def lanes_of(s):
        return slice(128 * s, 128 * s + 128)

    def prepare(store):
        for s in range(8):
            store_halves(0, lanes_of(s), flat(store)[pl.ds(s, total, stride=8), :], (0,), 1)

    prepare(sd6)
    weigh(1)

    def tier_four_came(q, carry):
        here(sds4.at[:, chunk(q), me], own_parts.at[0, q])
        arrived(sds4.at[:, chunk(q), others], part_sems.at[0, q])
        at = pl.multiple_of(q * rows_part, rows_part)
        wr = above_weights[0, pl.ds(at, rows_part), :]
        wi = above_weights[1, pl.ds(at, rows_part), :]
        for s in range(8):
            spread = pl.ds(at * 8 + s, rows_part, stride=8)
            c = flat(sds4.at[0])[spread, :]
            a = flat(sds4.at[1])[spread, :]
            flat(m4)[spread, :] = wr * c - wi * a
            store_halves(at, lanes_of(s), c, (2, 4), 3)
            store_halves(at, lanes_of(s), a, (5, 7), 6)
        remote(m4.at[chunk(q)], m4y.at[chunk(q)], 7, part_sems.at[1, q], (above, me)).start()
        return carry

    lax.fori_loop(0, PARTS, tier_four_came, 0)

    def combine(tier, store):
        for pair in range(4):
            lanes = slice(256 * pair, 256 * pair + 256)
            a = mxu(weights[tier], stack[:, lanes])
            for t in range(2):
                store(2 * pair + t, a[:, 128 * t : 128 * t + 128])

    def keep(s, value):
        drive[s] = value

    combine(0, keep)

    def send_home(sums, got, q, k, row):
        pltpu.make_async_copy(
            sums.at[chunk(q), me], got.at[chunk(q), tile(me), :], own_parts.at[row - 1, q]
        ).start()

        def fn(d):
            remote(
                sums.at[chunk(q), d],
                got.at[chunk(q), tile(me), :],
                k,
                part_sems.at[row, q],
                (ma, d),
            ).start()

        each_peer(fn)

    def got_home(got, q, row):
        here(got.at[chunk(q), tile(me), :], own_parts.at[row - 1, q])
        arrived(got.at[chunk(q), pl.ds(0, 8 * (peers - 1)), :], part_sems.at[row, q])

    arrived(d6y, recv_sems.at[4])

    def solve_five(q, carry):
        arrived(m4y.at[chunk(q)], part_sems.at[1, q])
        at = pl.multiple_of(q * rows_part, rows_part)
        some = pl.ds(at, rows_part)
        damping = damp_all[some, :]
        for t in range(4):
            gap = split_sq[0, pl.ds(me * 4 + t, 1), :]
            inverse = 1.0 / (damping * damping + gap * gap)
            factor_real = -damping * inverse
            factor_imag = gap * inverse
            value = []
            for s in (2 * t, 2 * t + 1):
                spread = pl.ds(at * 8 + s, rows_part, stride=8)
                value.append(drive[s, some, :] + flat(d6y)[spread, :] + flat(m4y)[spread, :])
            real = value[0] * factor_real - value[1] * factor_imag
            imag = value[0] * factor_imag + value[1] * factor_real
            for s, v in ((2 * t, real), (2 * t + 1, imag)):
                solved[s, some, :] = v
                flat(sums5)[pl.ds(at * 8 + s, rows_part, stride=8), :] = v
        send_home(sums5, got5, q, 8, 2)
        return carry

    lax.fori_loop(0, PARTS, solve_five, 0)

    def turn(s, carry):
        turned_by[s] = dot3(halves(solved[s]), const(coupled_at))
        return carry

    lax.fori_loop(0, 8, turn, 0)

    def whole(real, imag):
        y = jnp.concatenate([real, imag], axis=0)
        return dot3(const(basis_at), halves(beside(dot3(halves(y), const(turned_at)))))

    def tier_five(q, carry):
        got_home(got5, q, 2)
        remote(got5.at[chunk(q)], y5.at[chunk(q)], 9, part_sems.at[4, q], (above, me)).start()
        for r in range(part):
            m = q * part + r
            y = jnp.concatenate([got5[m, EVEN, :], got5[m, ODD, :]], axis=1)
            p = dot3(const(coupled_at), halves(y))
            p5[m, EVEN, :] = p[:, 0:128]
            p5[m, ODD, :] = p[:, 128:256]
        scatter(p5, sp5, 10, recv_sems.at[6], chunk(q))
        pltpu.make_async_copy(
            p5.at[chunk(q), tile(me), :], sp5.at[chunk(q), me], own_sems.at[6]
        ).start()
        for r in range(part):
            m = q * part + r
            back = whole(got5[m, EVEN, :], got5[m, ODD, :])
            out5[m, 0:128, :] = back[:, 0:128]
            out5[m, 128:256, :] = back[:, 128:256]
        return carry

    lax.fori_loop(0, PARTS, tier_five, 0)

    here(sd7.at[:, me], own_sems.at[5])
    arrived(sd7.at[:, others], recv_sems.at[2])
    prepare(sd7)
    here(sp5.at[:, me], own_sems.at[6])
    arrived(sp5.at[:, others], recv_sems.at[6])
    for t in range(4):
        p = [flat(sp5)[pl.ds(s, total, stride=8), :] for s in (2 * t, 2 * t + 1)]
        q = [turned_by[s] for s in (2 * t, 2 * t + 1)]
        store_halves(0, lanes_of(2 * t), q[1] - p[1], (2, 4), 3)
        store_halves(0, lanes_of(2 * t + 1), p[0] - q[0], (2, 4), 3)
        store_halves(0, lanes_of(2 * t), p[0] + q[0], (5, 7), 6)
        store_halves(0, lanes_of(2 * t + 1), p[1] + q[1], (5, 7), 6)

    def spread_out(s, value):
        flat(sums6)[pl.ds(s, total, stride=8), :] = value

    combine(1, spread_out)

    def home_six(q, carry):
        send_home(sums6, got6, q, 11, 3)
        return carry

    lax.fori_loop(0, PARTS, home_six, 0)

    arrived(d7y, recv_sems.at[5])

    def first_mode(q, carry):
        arrived(y5.at[chunk(q)], part_sems.at[4, q])
        for r in range(part):
            m = q * part + r
            real, imag = y5[m, EVEN, :], y5[m, ODD, :]
            p = dot3(const(coupled_at), halves(jnp.concatenate([real, imag], axis=1)))
            s = beside(
                dot3(halves(jnp.concatenate([real, imag], axis=0)), const(coupled_at))
            )
            c, a = p - s, p + s
            wr = rates[0, pl.ds(m, 1), :]
            wi = rates[1, pl.ds(m, 1), :]
            z6[m, 0:128, :] = d7y[m, EVEN, :] - wr * c[:, 128:256] - wi * a[:, 0:128]
            z6[m, 128:256, :] = d7y[m, ODD, :] + wr * c[:, 0:128] - wi * a[:, 128:256]
        return carry

    lax.fori_loop(0, PARTS, first_mode, 0)

    def tier_six(q, carry):
        got_home(got6, q, 3)
        for r in range(part):
            m = q * part + r
            damping = jnp.broadcast_to(rates[2, pl.ds(m, 1), :], (128, 128))
            inverse = 1.0 / (damping * damping + split_sq[1])
            factor_real = -damping * inverse
            factor_imag = split_sq[0] * inverse
            real = got6[m, EVEN, :] + z6[m, 0:128, :]
            imag = got6[m, ODD, :] + z6[m, 128:256, :]
            back = whole(
                real * factor_real - imag * factor_imag, real * factor_imag + imag * factor_real
            )
            out6[m, 0:128, :] = back[:, 0:128]
            out6[m, 128:256, :] = back[:, 128:256]
        return carry

    lax.fori_loop(0, PARTS, tier_six, 0)

    sent(tab.at[pl.ds(0, total - block)], 0)
    sent(sd6.at[:, others], 1)
    sent(sds4.at[:, :, others], 2)
    sent(sd7.at[:, others], 3)
    sent(tab, 4)
    sent(sd6, 5)
    sent(d7, 6)
    sent(m4, 7)
    sent(sums5.at[:, others], 8)
    sent(got5, 9)
    sent(sp5.at[:, others], 10)
    sent(sums6.at[:, others], 11)


def body(
    rows,
    peers,
    tier_four,
    tier_six,
    tier_seven,
    coupling,
    eigenbasis,
    energies,
    decay_rates,
    bath_coefficients,
    occupation_five,
    local_five,
    peers_five,
    places_five,
    occupation_six,
    local_six,
    peers_six,
    places_six,
):
    block = tier_four.shape[0]
    total = peers * block
    shape = tier_four.shape
    flat = (block, 256, 128)
    hbm = pl.BlockSpec(memory_space=pltpu.HBM)
    small = (
        coupling,
        eigenbasis,
        energies.reshape(1, -1),
        decay_rates.reshape(1, -1),
        bath_coefficients,
        occupation_five,
        local_five,
        peers_five.T,
        places_five.T,
        occupation_six,
        local_six,
        peers_six.T,
        places_six.T,
    )
    whole = pltpu.VMEM(flat, F32)
    pair = pltpu.VMEM((2,) + flat, F32)
    store = pltpu.VMEM((block, peers, 8, 128), F32)
    pair_store = pltpu.VMEM((2, block, peers, 8, 128), F32)
    slices = pltpu.VMEM((8, total, 128), F32)
    table = pltpu.VMEM((total, 128), F32)
    dma = pltpu.SemaphoreType.DMA
    five, six = pl.pallas_call(
        functools.partial(sweep_kernel, peers, rows, block),
        out_shape=(pltpu.VMEM(flat, F32), pltpu.VMEM(flat, F32)),
        in_specs=[hbm] * (3 + len(small)),
        scratch_shapes=[pltpu.VMEM(a.shape, a.dtype) for a in small]
        + [
            pltpu.VMEM((block, 128), F32),
            table,
            table,
            pltpu.VMEM((3,) + flat, F32),
            whole,
            pair,
            whole,
            whole,
            store,
            pair_store,
            store,
            store,
            store,
            store,
            store,
            whole,
            whole,
            whole,
            whole,
            store,
            store,
            slices,
            slices,
            slices,
            whole,
            pltpu.VMEM((2, total, 128), F32),
            table,
            pltpu.VMEM((2, total, 8 * total), BF16),
            pltpu.VMEM((8 * total, 1024), BF16),
            pltpu.VMEM((8, 128, 128), BF16),
            pltpu.VMEM((2, 128, 256), BF16),
            pltpu.VMEM((2, 128, 128), F32),
            pltpu.VMEM((3, block, 128), F32),
            dma((12,)),
            dma((7,)),
            dma((5, PARTS)),
            dma((7,)),
            dma((3, PARTS)),
            dma((N_SMALL,)),
        ],
        compiler_params=pltpu.CompilerParams(
            collective_id=0, has_side_effects=True, vmem_limit_bytes=64946176
        ),
        name="sweep",
    )(
        tier_four.reshape(flat),
        tier_six.reshape(flat),
        tier_seven.reshape(flat),
        *small,
    )
    return five.reshape(shape), six.reshape(shape)


def solution(mesh):
    rows, peers = mesh.shape["ma"], mesh.shape["mb"]
    whole = P(("ma", "mb"), None, None, None)
    wide = P(("ma", "mb"), None)
    tables = (wide, P(("ma", "mb"), None, None), wide, wide)
    in_specs = (whole,) * 3 + (P(),) * 5 + tables + tables
    return jax.shard_map(
        functools.partial(body, rows, peers),
        mesh=mesh,
        in_specs=in_specs,
        out_specs=(whole, whole),
        check_vma=False,
    )
```

```python
import functools

import jax
import jax.numpy as jnp
from jax import lax
from jax.experimental import pallas as pl
from jax.experimental.pallas import tpu as pltpu
from jax.sharding import PartitionSpec as P

MESH = pl.DeviceIdType.MESH
F32, BF16 = jnp.float32, jnp.bfloat16
PARTS = 4
STRIDE = 11
LOWER_AT, REAL_AT, IMAG_AT, DAMP_AT, TIER_AT = 11, 22, 34, 46, 64
N_SMALL = 13


def halves(x):
    high = x.astype(BF16)
    return high, (x - high.astype(F32)).astype(BF16)


def mxu(a, b):
    return jnp.dot(a, b, preferred_element_type=F32)


def dot3(a, b):
    return mxu(a[0], b[0]) + (mxu(a[0], b[1]) + mxu(a[1], b[0]))


def beside(x):
    return jnp.concatenate([x[0:128], x[128:256]], axis=1)


EVEN, ODD = pl.ds(0, 128, stride=2), pl.ds(1, 128, stride=2)


def sweep_kernel(peers, rows, block, x4, x6, x7, *refs):
    small, refs = refs[:N_SMALL], refs[N_SMALL:]
    out5, out6, *refs = refs
    local, refs = refs[:N_SMALL], refs[N_SMALL:]
    run(peers, rows, block, (x4, x6, x7), small, local, out5, out6, *refs)


def run(
    peers,
    rows,
    block,
    tiers,
    small,
    local,
    out5,
    out6,
    tab_in,
    tab,
    tab_above,
    held,
    d6,
    ds4,
    x7,
    sd6,
    sds4,
    sx7,
    m4,
    m4y,
    d6y,
    x7y,
    y5,
    got5,
    got6,
    sums5,
    sums6,
    drive,
    solved,
    z6,
    above_weights,
    damp_all,
    weights,
    stack,
    wide,
    both_right,
    split_sq,
    rates,
    send_sems,
    recv_sems,
    part_sems,
    own_sems,
    own_parts,
    home_recv,
    home_own,
    small_sems,
):
    total = peers * block
    part = block // PARTS
    rows_part = part * peers
    ma, me = lax.axis_index("ma"), lax.axis_index("mb")
    above = lax.rem(ma + 1, rows)
    below = lax.rem(ma + rows - 1, rows)

    def each_peer(fn):
        def step(j, carry):
            fn(lax.rem(me + lax.rem(j * STRIDE, peers), peers))
            return carry

        lax.fori_loop(1, peers, step, 0)

    def tile(d):
        return pl.ds(pl.multiple_of(d * 8, 8), 8)

    def chunk(q):
        return pl.ds(pl.multiple_of(q * part, part), part)

    others = pl.ds(0, peers - 1)

    def remote(src, dst, k, recv, device):
        return pltpu.make_async_remote_copy(
            src_ref=src,
            dst_ref=dst,
            send_sem=send_sems.at[k],
            recv_sem=recv,
            device_id=device,
            device_id_type=MESH,
        )

    def arrived(ref, recv):
        remote(ref, ref, 0, recv, (above, me)).wait_recv()

    def sent(ref, k):
        remote(ref, ref, k, recv_sems.at[0], (above, me)).wait_send()

    def here(ref, sem):
        pltpu.make_async_copy(ref, ref, sem).wait()

    def flat(ref):
        return ref.reshape(total * 8, 128)

    barrier = pltpu.get_barrier_semaphore()
    each_peer(lambda d: pl.semaphore_signal(barrier, inc=1, device_id=(ma, d), device_id_type=MESH))
    pl.semaphore_signal(barrier, inc=1, device_id=(above, me), device_id_type=MESH)
    pl.semaphore_signal(barrier, inc=1, device_id=(below, me), device_id_type=MESH)

    fetch = [
        pltpu.make_async_copy(a, b, small_sems.at[i]) for i, (a, b) in enumerate(zip(small, local))
    ]
    for copy in fetch:
        copy.start()
    load = [pltpu.make_async_copy(a, held.at[i], own_sems.at[1 + i]) for i, a in enumerate(tiers)]
    for i in (1, 0, 2):
        load[i].start()
    coupling, basis, energies, decay, bath, *tables = local

    for copy in fetch:
        copy.wait()
    lane = lax.broadcasted_iota(jnp.int32, (block, 128), 1)
    on_diagonal = lax.broadcasted_iota(jnp.int32, (block, block), 0) == lax.broadcasted_iota(
        jnp.int32, (block, block), 1
    )
    entries = jnp.zeros((block, 128), F32)

    def put(entries, at, column):
        return jnp.where(lane == at, jnp.broadcast_to(column, (block, 128)), entries)

    for tier in range(2):
        occupation, near, peer_ids, places = tables[4 * tier : 4 * tier + 4]
        base = tier * TIER_AT
        wanted = (places[...] * peers + peer_ids[...]).astype(F32)
        for k in range(4):
            row = jnp.broadcast_to(wanted[k : k + 1, :], (block, block))
            column = jnp.sum(jnp.where(on_diagonal, row, 0.0), axis=1, keepdims=True)
            entries = put(entries, base + (k if k < 2 else LOWER_AT + k - 2), column)
        inside = (near[...] * peers + me).astype(F32)
        up, low = inside[:, 0, :], inside[:, 1, :]
        for k in range(9):
            entries = put(entries, base + 2 + k, up[:, k : k + 1])
            entries = put(entries, base + LOWER_AT + 2 + k, low[:, k : k + 1])
        counted = occupation[...].astype(F32)
        real = counted * bath[0:1, :]
        imag = counted * bath[1:2, :]
        for k in range(12):
            entries = put(entries, base + REAL_AT + k, real[:, k : k + 1])
            entries = put(entries, base + IMAG_AT + k, imag[:, k : k + 1])
        damp = jnp.sum(counted * decay[...], axis=1, keepdims=True)
        entries = put(entries, base + DAMP_AT, damp)
    for spot, column in enumerate((real[:, 0:1], imag[:, 0:1], damp)):
        rates[spot] = jnp.broadcast_to(column, (block, 128))
    tab_in[...] = entries
    mine = pl.ds(pl.multiple_of(me * block, block), block)
    own_tab = pltpu.make_async_copy(tab_in, tab.at[mine], own_sems.at[0])
    own_tab.start()

    e = basis[...]
    turned = jnp.transpose(e)
    e2, c2, t2 = halves(e), halves(coupling[...]), halves(turned)
    wide[0], wide[1] = e2
    wide[2], wide[3] = t2
    ce = halves(dot3(c2, e2))
    wide[4], wide[5] = halves(dot3(t2, ce))
    wide[6], wide[7] = halves(dot3(t2, c2))
    for i in range(2):
        both_right[i, :, 0:128] = e2[i]
        both_right[i, :, 128:256] = ce[i]
    across = jnp.broadcast_to(energies[...], (128, 128))
    split = jnp.transpose(across) - across
    split_sq[0] = split
    split_sq[1] = split * split

    def const(k):
        return wide[2 * k], wide[2 * k + 1]

    basis_at, turned_at, coupled_at, from_left_at = 0, 1, 2, 3

    def products(x):
        t = dot3(halves(x), (both_right[0], both_right[1]))
        left = dot3(const(from_left_at), halves(beside(t[:, 0:128])))
        right = dot3(const(turned_at), halves(beside(t[:, 128:256])))
        return left, right

    def put_commutator(ref, p, q):
        c = p - q
        ref[EVEN, :] = -c[:, 128:256]
        ref[ODD, :] = c[:, 0:128]

    def commutators(which, out, first, count):
        def step(m, carry):
            p, q = products(held[which, m])
            put_commutator(out.at[m], p, q)
            return carry

        lax.fori_loop(first, first + count, step, 0)

    def scatter(src, dst, k, recv, some):
        def fn(d):
            remote(src.at[some, tile(d), :], dst.at[some, me], k, recv, (ma, d)).start()

        each_peer(fn)

    half = block // 2
    load[1].wait()
    commutators(1, d6, 0, half)
    pl.semaphore_wait(barrier, peers + 1)
    each_peer(lambda d: remote(tab_in, tab.at[mine], 0, recv_sems.at[0], (ma, d)).start())
    scatter(d6, sd6, 1, recv_sems.at[1], pl.ds(0, half))
    commutators(1, d6, half, half)
    scatter(d6, sd6, 1, recv_sems.at[1], pl.ds(half, half))
    everything = pl.ds(0, block)
    pltpu.make_async_copy(d6.at[:, tile(me), :], sd6.at[:, me], own_sems.at[4]).start()

    load[0].wait()

    def tier_four(q, carry):
        for r in range(part):
            m = q * part + r
            p, s = products(held[0, m])
            put_commutator(ds4.at[0, m], p, s)
            both = p + s
            ds4[1, m, EVEN, :] = both[:, 0:128]
            ds4[1, m, ODD, :] = both[:, 128:256]

        def fn(d):
            remote(
                ds4.at[:, chunk(q), tile(d), :],
                sds4.at[:, chunk(q), me],
                2,
                part_sems.at[0, q],
                (ma, d),
            ).start()

        each_peer(fn)
        pltpu.make_async_copy(
            ds4.at[:, chunk(q), tile(me), :], sds4.at[:, chunk(q), me], own_parts.at[0, q]
        ).start()
        return carry

    lax.fori_loop(0, PARTS, tier_four, 0)

    load[2].wait()

    def tier_seven(m, carry):
        t = beside(dot3(halves(held[2, m]), const(basis_at)))
        x = dot3(const(turned_at), halves(t))
        x7[m, EVEN, :] = x[:, 0:128]
        x7[m, ODD, :] = x[:, 128:256]
        return carry

    lax.fori_loop(0, block, tier_seven, 0)
    scatter(x7, sx7, 3, recv_sems.at[2], everything)
    pltpu.make_async_copy(x7.at[:, tile(me), :], sx7.at[:, me], own_sems.at[5]).start()

    own_tab.wait()
    arrived(tab.at[pl.ds(0, total - block)], recv_sems.at[0])
    remote(tab, tab_above, 4, recv_sems.at[3], (below, me)).start()
    here(sd6.at[:, me], own_sems.at[4])
    arrived(sd6.at[:, others], recv_sems.at[1])
    remote(sd6, d6y, 5, recv_sems.at[4], (below, me)).start()
    remote(x7, x7y, 6, recv_sems.at[5], (below, me)).start()

    def weigh(tier):
        base = tier * TIER_AT

        def step(i, carry):
            at = pl.ds(pl.multiple_of(i * peers, peers), peers)
            t = tab[pl.ds(i, peers, stride=block), :]
            column = lax.broadcasted_iota(jnp.int32, (peers, total), 1).astype(F32)
            up = jnp.zeros((peers, total), F32)
            real = jnp.zeros((peers, total), F32)
            imag = jnp.zeros((peers, total), F32)
            for k in range(11):
                hit = t[:, base + k : base + k + 1] == column
                up = up + jnp.where(hit, 1.0, 0.0)
                hit = t[:, base + LOWER_AT + k : base + LOWER_AT + k + 1] == column
                wr = t[:, base + REAL_AT + k + 1 : base + REAL_AT + k + 2]
                wi = t[:, base + IMAG_AT + k + 1 : base + IMAG_AT + k + 2]
                real = real + jnp.where(hit, wr, 0.0)
                imag = imag + jnp.where(hit, wi, 0.0)
            rh, rl = halves(real)
            ih, il = halves(-imag if tier == 0 else imag)
            u = up.astype(BF16)
            for spot, value in enumerate((u, u, rh, rh, rl, ih, ih, il)):
                weights[tier, at, spot * total : (spot + 1) * total] = value
            if tier == 0:
                damp_all[at, :] = jnp.broadcast_to(t[:, DAMP_AT : DAMP_AT + 1], (peers, 128))
            return carry

        lax.fori_loop(0, block, step, 0)

    weigh(0)
    arrived(tab_above, recv_sems.at[3])

    def next_row(i, carry):
        at = pl.ds(pl.multiple_of(i * peers, peers), peers)
        t = tab_above[pl.ds(i, peers, stride=block), :]
        above_weights[0, at, :] = jnp.broadcast_to(t[:, REAL_AT : REAL_AT + 1], (peers, 128))
        above_weights[1, at, :] = jnp.broadcast_to(t[:, IMAG_AT : IMAG_AT + 1], (peers, 128))
        return carry

    lax.fori_loop(0, block, next_row, 0)

    def store_halves(at, lanes, value, spots_high, spot_low):
        high, low = halves(value)
        for spot in spots_high:
            stack[pl.ds(at + spot * total, value.shape[0]), lanes] = high
        stack[pl.ds(at + spot_low * total, value.shape[0]), lanes] = low

    def lanes_of(s):
        return slice(128 * s, 128 * s + 128)

    def prepare(store):
        for s in range(8):
            store_halves(0, lanes_of(s), flat(store)[pl.ds(s, total, stride=8), :], (0,), 1)

    prepare(sd6)
    weigh(1)

    def tier_four_came(q, carry):
        here(sds4.at[:, chunk(q), me], own_parts.at[0, q])
        arrived(sds4.at[:, chunk(q), others], part_sems.at[0, q])
        at = pl.multiple_of(q * rows_part, rows_part)
        wr = above_weights[0, pl.ds(at, rows_part), :]
        wi = above_weights[1, pl.ds(at, rows_part), :]
        for s in range(8):
            spread = pl.ds(at * 8 + s, rows_part, stride=8)
            c = flat(sds4.at[0])[spread, :]
            a = flat(sds4.at[1])[spread, :]
            flat(m4)[spread, :] = wr * c - wi * a
            store_halves(at, lanes_of(s), c, (2, 4), 3)
            store_halves(at, lanes_of(s), a, (5, 7), 6)
        remote(m4.at[chunk(q)], m4y.at[chunk(q)], 7, part_sems.at[1, q], (above, me)).start()
        return carry

    lax.fori_loop(0, PARTS, tier_four_came, 0)

    def lanes_of_pair(pair):
        return slice(256 * pair, 256 * pair + 256)

    for pair in range(4):
        a = mxu(weights[0], stack[:, lanes_of_pair(pair)])
        drive[2 * pair] = a[:, 0:128]
        drive[2 * pair + 1] = a[:, 128:256]

    def send_home(src_of, got, where, k, own, recv):
        pltpu.make_async_copy(src_of(me), got.at[where + (tile(me),)], own).start()

        def fn(d):
            remote(src_of(d), got.at[where + (tile(me),)], k, recv, (ma, d)).start()

        each_peer(fn)

    def got_home(got, where, own, recv):
        here(got.at[where + (tile(me),)], own)
        arrived(got.at[where + (pl.ds(0, 8 * (peers - 1)),)], recv)

    arrived(d6y, recv_sems.at[4])

    def solve_five(q, carry):
        arrived(m4y.at[chunk(q)], part_sems.at[1, q])
        at = pl.multiple_of(q * rows_part, rows_part)
        some = pl.ds(at, rows_part)
        damping = damp_all[some, :]
        for t in range(4):
            gap = split_sq[0, pl.ds(me * 4 + t, 1), :]
            inverse = 1.0 / (damping * damping + gap * gap)
            factor_real = -damping * inverse
            factor_imag = gap * inverse
            value = []
            for s in (2 * t, 2 * t + 1):
                spread = pl.ds(at * 8 + s, rows_part, stride=8)
                value.append(drive[s, some, :] + flat(d6y)[spread, :] + flat(m4y)[spread, :])
            real = value[0] * factor_real - value[1] * factor_imag
            imag = value[0] * factor_imag + value[1] * factor_real
            for s, v in ((2 * t, real), (2 * t + 1, imag)):
                solved[s, some, :] = v
                flat(sums5)[pl.ds(at * 8 + s, rows_part, stride=8), :] = v
        send_home(
            lambda d: sums5.at[chunk(q), d],
            got5,
            (chunk(q),),
            8,
            own_parts.at[1, q],
            part_sems.at[2, q],
        )
        return carry

    lax.fori_loop(0, PARTS, solve_five, 0)

    def whole(real, imag):
        y = jnp.concatenate([real, imag], axis=0)
        return dot3(const(basis_at), halves(beside(dot3(halves(y), const(turned_at)))))

    here(sx7.at[:, me], own_sems.at[5])
    arrived(sx7.at[:, others], recv_sems.at[2])
    prepare(sx7)
    for s in range(8):
        store_halves(0, lanes_of(s), solved[s], (2, 4), 3)
    for t in range(4):
        a = mxu(weights[1, :, 0 : 5 * total], stack[0 : 5 * total, lanes_of_pair(t)])
        b = mxu(weights[1, :, 5 * total :], stack[2 * total : 5 * total, lanes_of_pair(t)])
        ar, ai, br, bi = a[:, 0:128], a[:, 128:256], b[:, 0:128], b[:, 128:256]
        other = dot3(
            halves(jnp.concatenate([ar + bi, ai - br], axis=0)), const(coupled_at)
        )
        for r, value in enumerate((ar - bi, ai + br)):
            spread = pl.ds(2 * t + r, total, stride=8)
            flat(sums6.at[0])[spread, :] = value
            flat(sums6.at[1])[spread, :] = other[r * total : (r + 1) * total]

    def home_six(q, carry):
        send_home(
            lambda d: sums6.at[:, q, d],
            got6,
            (slice(None), q),
            10,
            home_own.at[q],
            home_recv.at[q],
        )
        return carry

    lax.fori_loop(0, block, home_six, 0)

    def tier_five(q, carry):
        got_home(got5, (chunk(q),), own_parts.at[1, q], part_sems.at[2, q])
        remote(got5.at[chunk(q)], y5.at[chunk(q)], 9, part_sems.at[3, q], (above, me)).start()
        for r in range(part):
            m = q * part + r
            back = whole(got5[m, EVEN, :], got5[m, ODD, :])
            out5[m, 0:128, :] = back[:, 0:128]
            out5[m, 128:256, :] = back[:, 128:256]
        return carry

    lax.fori_loop(0, PARTS, tier_five, 0)

    arrived(x7y, recv_sems.at[5])

    def first_mode(q):
        arrived(y5.at[chunk(q)], part_sems.at[3, q])
        for r in range(part):
            m = q * part + r
            real, imag = y5[m, EVEN, :], y5[m, ODD, :]
            wr = rates[0, pl.ds(m, 1), :]
            wi = rates[1, pl.ds(m, 1), :]
            ar, ai = x7y[m, EVEN, :] + wr * real, x7y[m, ODD, :] + wr * imag
            br, bi = wi * real, wi * imag
            z6[0, m] = jnp.concatenate([ar - bi, ai + br], axis=0)
            z6[1, m] = dot3(
                halves(jnp.concatenate([ar + bi, ai - br], axis=0)), const(coupled_at)
            )

    def tier_six(m):
        got_home(got6, (slice(None), m), home_own.at[m], home_recv.at[m])
        pair = jnp.concatenate(
            [got6[0, m, EVEN, :] + z6[0, m, 0:128], got6[0, m, ODD, :] + z6[0, m, 128:256]], axis=1
        )
        other = jnp.concatenate(
            [got6[1, m, EVEN, :] + z6[1, m, 0:128], got6[1, m, ODD, :] + z6[1, m, 128:256]], axis=1
        )
        comm = dot3(const(coupled_at), halves(pair)) - other
        real, imag = -comm[:, 128:256], comm[:, 0:128]
        damping = jnp.broadcast_to(rates[2, pl.ds(m, 1), :], (128, 128))
        inverse = 1.0 / (damping * damping + split_sq[1])
        factor_real = -damping * inverse
        factor_imag = split_sq[0] * inverse
        back = whole(
            real * factor_real - imag * factor_imag, real * factor_imag + imag * factor_real
        )
        out6[m, 0:128, :] = back[:, 0:128]
        out6[m, 128:256, :] = back[:, 128:256]

    def finish(q, carry):
        first_mode(q)
        for r in range(part):
            tier_six(q * part + r)
        return carry

    lax.fori_loop(0, PARTS, finish, 0)

    sent(tab.at[pl.ds(0, total - block)], 0)
    sent(sd6.at[:, others], 1)
    sent(sds4.at[:, :, others], 2)
    sent(sx7.at[:, others], 3)
    sent(tab, 4)
    sent(sd6, 5)
    sent(x7, 6)
    sent(m4, 7)
    sent(sums5.at[:, others], 8)
    sent(got5, 9)
    sent(sums6.at[:, :, others], 10)


def body(
    rows,
    peers,
    tier_four,
    tier_six,
    tier_seven,
    coupling,
    eigenbasis,
    energies,
    decay_rates,
    bath_coefficients,
    occupation_five,
    local_five,
    peers_five,
    places_five,
    occupation_six,
    local_six,
    peers_six,
    places_six,
):
    block = tier_four.shape[0]
    total = peers * block
    shape = tier_four.shape
    flat = (block, 256, 128)
    hbm = pl.BlockSpec(memory_space=pltpu.HBM)
    small = (
        coupling,
        eigenbasis,
        energies.reshape(1, -1),
        decay_rates.reshape(1, -1),
        bath_coefficients,
        occupation_five,
        local_five,
        peers_five.T,
        places_five.T,
        occupation_six,
        local_six,
        peers_six.T,
        places_six.T,
    )
    whole = pltpu.VMEM(flat, F32)
    pair = pltpu.VMEM((2,) + flat, F32)
    store = pltpu.VMEM((block, peers, 8, 128), F32)
    pair_store = pltpu.VMEM((2, block, peers, 8, 128), F32)
    slices = pltpu.VMEM((8, total, 128), F32)
    table = pltpu.VMEM((total, 128), F32)
    dma = pltpu.SemaphoreType.DMA
    five, six = pl.pallas_call(
        functools.partial(sweep_kernel, peers, rows, block),
        out_shape=(pltpu.VMEM(flat, F32), pltpu.VMEM(flat, F32)),
        in_specs=[hbm] * (3 + len(small)),
        scratch_shapes=[pltpu.VMEM(a.shape, a.dtype) for a in small]
        + [
            pltpu.VMEM((block, 128), F32),
            table,
            table,
            pltpu.VMEM((3,) + flat, F32),
            whole,
            pair,
            whole,
            store,
            pair_store,
            store,
            store,
            store,
            store,
            whole,
            whole,
            whole,
            pair,
            store,
            pair_store,
            slices,
            slices,
            pair,
            pltpu.VMEM((2, total, 128), F32),
            table,
            pltpu.VMEM((2, total, 8 * total), BF16),
            pltpu.VMEM((8 * total, 1024), BF16),
            pltpu.VMEM((8, 128, 128), BF16),
            pltpu.VMEM((2, 128, 256), BF16),
            pltpu.VMEM((2, 128, 128), F32),
            pltpu.VMEM((3, block, 128), F32),
            dma((11,)),
            dma((6,)),
            dma((4, PARTS)),
            dma((6,)),
            dma((2, PARTS)),
            dma((block,)),
            dma((block,)),
            dma((N_SMALL,)),
        ],
        compiler_params=pltpu.CompilerParams(
            collective_id=0, has_side_effects=True, vmem_limit_bytes=64946176
        ),
        name="sweep",
    )(
        tier_four.reshape(flat),
        tier_six.reshape(flat),
        tier_seven.reshape(flat),
        *small,
    )
    return five.reshape(shape), six.reshape(shape)


def solution(mesh):
    rows, peers = mesh.shape["ma"], mesh.shape["mb"]
    whole = P(("ma", "mb"), None, None, None)
    wide = P(("ma", "mb"), None)
    tables = (wide, P(("ma", "mb"), None, None), wide, wide)
    in_specs = (whole,) * 3 + (P(),) * 5 + tables + tables
    return jax.shard_map(
        functools.partial(body, rows, peers),
        mesh=mesh,
        in_specs=in_specs,
        out_specs=(whole, whole),
        check_vma=False,
    )
```

```python
import functools

import jax
import jax.numpy as jnp
from jax import lax
from jax.experimental import pallas as pl
from jax.experimental.pallas import tpu as pltpu
from jax.sharding import PartitionSpec as P

MESH = pl.DeviceIdType.MESH
F32, BF16 = jnp.float32, jnp.bfloat16
PARTS = 4
STRIDE = 5
LOWER_AT, REAL_AT, IMAG_AT, DAMP_AT, TIER_AT = 11, 22, 34, 46, 64
N_SMALL = 13


def halves(x):
    high = x.astype(BF16)
    return high, (x - high.astype(F32)).astype(BF16)


def mxu(a, b):
    return jnp.dot(a, b, preferred_element_type=F32)


def dot3(a, b):
    return mxu(a[0], b[0]) + (mxu(a[0], b[1]) + mxu(a[1], b[0]))


def beside(x):
    return jnp.concatenate([x[0:128], x[128:256]], axis=1)


EVEN, ODD = pl.ds(0, 128, stride=2), pl.ds(1, 128, stride=2)


def sweep_kernel(peers, rows, block, x4, x6, x7, *refs):
    small, refs = refs[:N_SMALL], refs[N_SMALL:]
    out5, out6, *refs = refs
    local, refs = refs[:N_SMALL], refs[N_SMALL:]
    run(peers, rows, block, (x4, x6, x7), small, local, out5, out6, *refs)


def run(
    peers,
    rows,
    block,
    tiers,
    small,
    local,
    out5,
    out6,
    tab_in,
    tab,
    tab_above,
    held,
    d6,
    ds4,
    x7,
    sd6,
    sds4,
    sx7,
    m4,
    m4y,
    d6y,
    x7y,
    y5,
    got5,
    got6,
    sums5,
    sums6,
    drive,
    solved,
    z6,
    above_weights,
    damp_all,
    weights,
    stack,
    wide,
    both_right,
    split_sq,
    rates,
    send_sems,
    recv_sems,
    part_sems,
    own_sems,
    own_parts,
    home_recv,
    home_own,
    small_sems,
):
    total = peers * block
    part = block // PARTS
    rows_part = part * peers
    ma, me = lax.axis_index("ma"), lax.axis_index("mb")
    above = lax.rem(ma + 1, rows)
    below = lax.rem(ma + rows - 1, rows)

    def each_peer(fn):
        def step(j, carry):
            fn(lax.rem(me + lax.rem(j * STRIDE, peers), peers))
            return carry

        lax.fori_loop(1, peers, step, 0)

    def tile(d):
        return pl.ds(pl.multiple_of(d * 8, 8), 8)

    def chunk(q):
        return pl.ds(pl.multiple_of(q * part, part), part)

    others = pl.ds(0, peers - 1)

    def remote(src, dst, k, recv, device):
        return pltpu.make_async_remote_copy(
            src_ref=src,
            dst_ref=dst,
            send_sem=send_sems.at[k],
            recv_sem=recv,
            device_id=device,
            device_id_type=MESH,
        )

    def arrived(ref, recv):
        remote(ref, ref, 0, recv, (above, me)).wait_recv()

    def sent(ref, k):
        remote(ref, ref, k, recv_sems.at[0], (above, me)).wait_send()

    def here(ref, sem):
        pltpu.make_async_copy(ref, ref, sem).wait()

    def flat(ref):
        return ref.reshape(total * 8, 128)

    barrier = pltpu.get_barrier_semaphore()
    each_peer(lambda d: pl.semaphore_signal(barrier, inc=1, device_id=(ma, d), device_id_type=MESH))
    pl.semaphore_signal(barrier, inc=1, device_id=(above, me), device_id_type=MESH)
    pl.semaphore_signal(barrier, inc=1, device_id=(below, me), device_id_type=MESH)

    fetch = [
        pltpu.make_async_copy(a, b, small_sems.at[i]) for i, (a, b) in enumerate(zip(small, local))
    ]
    for copy in fetch:
        copy.start()
    load = [pltpu.make_async_copy(a, held.at[i], own_sems.at[1 + i]) for i, a in enumerate(tiers)]
    for i in (1, 0, 2):
        load[i].start()
    coupling, basis, energies, decay, bath, *tables = local

    for copy in fetch:
        copy.wait()
    lane = lax.broadcasted_iota(jnp.int32, (block, 128), 1)
    on_diagonal = lax.broadcasted_iota(jnp.int32, (block, block), 0) == lax.broadcasted_iota(
        jnp.int32, (block, block), 1
    )
    entries = jnp.zeros((block, 128), F32)

    def put(entries, at, column):
        return jnp.where(lane == at, jnp.broadcast_to(column, (block, 128)), entries)

    for tier in range(2):
        occupation, near, peer_ids, places = tables[4 * tier : 4 * tier + 4]
        base = tier * TIER_AT
        wanted = (places[...] * peers + peer_ids[...]).astype(F32)
        for k in range(4):
            row = jnp.broadcast_to(wanted[k : k + 1, :], (block, block))
            column = jnp.sum(jnp.where(on_diagonal, row, 0.0), axis=1, keepdims=True)
            entries = put(entries, base + (k if k < 2 else LOWER_AT + k - 2), column)
        inside = (near[...] * peers + me).astype(F32)
        up, low = inside[:, 0, :], inside[:, 1, :]
        for k in range(9):
            entries = put(entries, base + 2 + k, up[:, k : k + 1])
            entries = put(entries, base + LOWER_AT + 2 + k, low[:, k : k + 1])
        counted = occupation[...].astype(F32)
        real = counted * bath[0:1, :]
        imag = counted * bath[1:2, :]
        for k in range(12):
            entries = put(entries, base + REAL_AT + k, real[:, k : k + 1])
            entries = put(entries, base + IMAG_AT + k, imag[:, k : k + 1])
        damp = jnp.sum(counted * decay[...], axis=1, keepdims=True)
        entries = put(entries, base + DAMP_AT, damp)
    for spot, column in enumerate((real[:, 0:1], imag[:, 0:1], damp)):
        rates[spot] = jnp.broadcast_to(column, (block, 128))
    tab_in[...] = entries
    mine = pl.ds(pl.multiple_of(me * block, block), block)
    own_tab = pltpu.make_async_copy(tab_in, tab.at[mine], own_sems.at[0])
    own_tab.start()

    e = basis[...]
    turned = jnp.transpose(e)
    e2, c2, t2 = halves(e), halves(coupling[...]), halves(turned)
    wide[0], wide[1] = e2
    wide[2], wide[3] = t2
    ce = halves(dot3(c2, e2))
    wide[4], wide[5] = halves(dot3(t2, ce))
    wide[6], wide[7] = halves(dot3(t2, c2))
    for i in range(2):
        both_right[i, :, 0:128] = e2[i]
        both_right[i, :, 128:256] = ce[i]
    across = jnp.broadcast_to(energies[...], (128, 128))
    split = jnp.transpose(across) - across
    split_sq[0] = split
    split_sq[1] = split * split

    def const(k):
        return wide[2 * k], wide[2 * k + 1]

    basis_at, turned_at, coupled_at, from_left_at = 0, 1, 2, 3

    def products(x):
        t = dot3(halves(x), (both_right[0], both_right[1]))
        left = dot3(const(from_left_at), halves(beside(t[:, 0:128])))
        right = dot3(const(turned_at), halves(beside(t[:, 128:256])))
        return left, right

    def put_commutator(ref, p, q):
        c = p - q
        ref[EVEN, :] = -c[:, 128:256]
        ref[ODD, :] = c[:, 0:128]

    def commutators(which, out, first, count):
        def step(m, carry):
            p, q = products(held[which, m])
            put_commutator(out.at[m], p, q)
            return carry

        lax.fori_loop(first, first + count, step, 0)

    def scatter(src, dst, k, recv, some):
        def fn(d):
            remote(src.at[some, tile(d), :], dst.at[some, me], k, recv, (ma, d)).start()

        each_peer(fn)

    half = block // 2
    load[1].wait()
    commutators(1, d6, 0, half)
    pl.semaphore_wait(barrier, peers + 1)
    each_peer(lambda d: remote(tab_in, tab.at[mine], 0, recv_sems.at[0], (ma, d)).start())
    scatter(d6, sd6, 1, recv_sems.at[1], pl.ds(0, half))
    commutators(1, d6, half, half)
    scatter(d6, sd6, 1, recv_sems.at[1], pl.ds(half, half))
    everything = pl.ds(0, block)
    pltpu.make_async_copy(d6.at[:, tile(me), :], sd6.at[:, me], own_sems.at[4]).start()

    load[0].wait()

    def tier_four(q, carry):
        for r in range(part):
            m = q * part + r
            p, s = products(held[0, m])
            put_commutator(ds4.at[0, m], p, s)
            both = p + s
            ds4[1, m, EVEN, :] = both[:, 0:128]
            ds4[1, m, ODD, :] = both[:, 128:256]

        def fn(d):
            remote(
                ds4.at[:, chunk(q), tile(d), :],
                sds4.at[:, chunk(q), me],
                2,
                part_sems.at[0, q],
                (ma, d),
            ).start()

        each_peer(fn)
        pltpu.make_async_copy(
            ds4.at[:, chunk(q), tile(me), :], sds4.at[:, chunk(q), me], own_parts.at[0, q]
        ).start()
        return carry

    lax.fori_loop(0, PARTS, tier_four, 0)

    load[2].wait()

    def tier_seven(m, carry):
        t = beside(dot3(halves(held[2, m]), const(basis_at)))
        x = dot3(const(turned_at), halves(t))
        x7[m, EVEN, :] = x[:, 0:128]
        x7[m, ODD, :] = x[:, 128:256]
        return carry

    lax.fori_loop(0, block, tier_seven, 0)
    scatter(x7, sx7, 3, recv_sems.at[2], everything)
    pltpu.make_async_copy(x7.at[:, tile(me), :], sx7.at[:, me], own_sems.at[5]).start()

    own_tab.wait()
    arrived(tab.at[pl.ds(0, total - block)], recv_sems.at[0])
    remote(tab, tab_above, 4, recv_sems.at[3], (below, me)).start()
    here(sd6.at[:, me], own_sems.at[4])
    arrived(sd6.at[:, others], recv_sems.at[1])
    remote(sd6, d6y, 5, recv_sems.at[4], (below, me)).start()
    remote(x7, x7y, 6, recv_sems.at[5], (below, me)).start()

    def weigh(tier):
        base = tier * TIER_AT

        def step(i, carry):
            at = pl.ds(pl.multiple_of(i * peers, peers), peers)
            t = tab[pl.ds(i, peers, stride=block), :]
            column = lax.broadcasted_iota(jnp.int32, (peers, total), 1).astype(F32)
            up = jnp.zeros((peers, total), F32)
            real = jnp.zeros((peers, total), F32)
            imag = jnp.zeros((peers, total), F32)
            for k in range(11):
                hit = t[:, base + k : base + k + 1] == column
                up = up + jnp.where(hit, 1.0, 0.0)
                hit = t[:, base + LOWER_AT + k : base + LOWER_AT + k + 1] == column
                wr = t[:, base + REAL_AT + k + 1 : base + REAL_AT + k + 2]
                wi = t[:, base + IMAG_AT + k + 1 : base + IMAG_AT + k + 2]
                real = real + jnp.where(hit, wr, 0.0)
                imag = imag + jnp.where(hit, wi, 0.0)
            rh, rl = halves(real)
            ih, il = halves(-imag if tier == 0 else imag)
            u = up.astype(BF16)
            for spot, value in enumerate((u, u, rh, rh, rl, ih, ih, il)):
                weights[tier, at, spot * total : (spot + 1) * total] = value
            if tier == 0:
                damp_all[at, :] = jnp.broadcast_to(t[:, DAMP_AT : DAMP_AT + 1], (peers, 128))
            return carry

        lax.fori_loop(0, block, step, 0)

    weigh(0)
    arrived(tab_above, recv_sems.at[3])

    def next_row(i, carry):
        at = pl.ds(pl.multiple_of(i * peers, peers), peers)
        t = tab_above[pl.ds(i, peers, stride=block), :]
        above_weights[0, at, :] = jnp.broadcast_to(t[:, REAL_AT : REAL_AT + 1], (peers, 128))
        above_weights[1, at, :] = jnp.broadcast_to(t[:, IMAG_AT : IMAG_AT + 1], (peers, 128))
        return carry

    lax.fori_loop(0, block, next_row, 0)

    def store_halves(at, lanes, value, spots_high, spot_low):
        high, low = halves(value)
        for spot in spots_high:
            stack[pl.ds(at + spot * total, value.shape[0]), lanes] = high
        stack[pl.ds(at + spot_low * total, value.shape[0]), lanes] = low

    def lanes_of(s):
        return slice(128 * s, 128 * s + 128)

    def prepare(store):
        for s in range(8):
            store_halves(0, lanes_of(s), flat(store)[pl.ds(s, total, stride=8), :], (0,), 1)

    prepare(sd6)
    weigh(1)

    def tier_four_came(q, carry):
        here(sds4.at[:, chunk(q), me], own_parts.at[0, q])
        arrived(sds4.at[:, chunk(q), others], part_sems.at[0, q])
        at = pl.multiple_of(q * rows_part, rows_part)
        wr = above_weights[0, pl.ds(at, rows_part), :]
        wi = above_weights[1, pl.ds(at, rows_part), :]
        for s in range(8):
            spread = pl.ds(at * 8 + s, rows_part, stride=8)
            c = flat(sds4.at[0])[spread, :]
            a = flat(sds4.at[1])[spread, :]
            flat(m4)[spread, :] = wr * c - wi * a
            store_halves(at, lanes_of(s), c, (2, 4), 3)
            store_halves(at, lanes_of(s), a, (5, 7), 6)
        remote(m4.at[chunk(q)], m4y.at[chunk(q)], 7, part_sems.at[1, q], (above, me)).start()
        return carry

    lax.fori_loop(0, PARTS, tier_four_came, 0)

    def lanes_of_pair(pair):
        return slice(256 * pair, 256 * pair + 256)

    for pair in range(4):
        a = mxu(weights[0], stack[:, lanes_of_pair(pair)])
        drive[2 * pair] = a[:, 0:128]
        drive[2 * pair + 1] = a[:, 128:256]

    def send_home(src_of, got, where, k, own, recv):
        pltpu.make_async_copy(src_of(me), got.at[where + (tile(me),)], own).start()

        def fn(d):
            remote(src_of(d), got.at[where + (tile(me),)], k, recv, (ma, d)).start()

        each_peer(fn)

    def got_home(got, where, own, recv):
        here(got.at[where + (tile(me),)], own)
        arrived(got.at[where + (pl.ds(0, 8 * (peers - 1)),)], recv)

    arrived(d6y, recv_sems.at[4])

    def solve_five(q, carry):
        arrived(m4y.at[chunk(q)], part_sems.at[1, q])
        at = pl.multiple_of(q * rows_part, rows_part)
        some = pl.ds(at, rows_part)
        damping = damp_all[some, :]
        for t in range(4):
            gap = split_sq[0, pl.ds(me * 4 + t, 1), :]
            inverse = 1.0 / (damping * damping + gap * gap)
            factor_real = -damping * inverse
            factor_imag = gap * inverse
            value = []
            for s in (2 * t, 2 * t + 1):
                spread = pl.ds(at * 8 + s, rows_part, stride=8)
                value.append(drive[s, some, :] + flat(d6y)[spread, :] + flat(m4y)[spread, :])
            real = value[0] * factor_real - value[1] * factor_imag
            imag = value[0] * factor_imag + value[1] * factor_real
            for s, v in ((2 * t, real), (2 * t + 1, imag)):
                solved[s, some, :] = v
                flat(sums5)[pl.ds(at * 8 + s, rows_part, stride=8), :] = v
        send_home(
            lambda d: sums5.at[chunk(q), d],
            got5,
            (chunk(q),),
            8,
            own_parts.at[1, q],
            part_sems.at[2, q],
        )
        return carry

    lax.fori_loop(0, PARTS, solve_five, 0)

    def whole(real, imag):
        y = jnp.concatenate([real, imag], axis=0)
        return dot3(const(basis_at), halves(beside(dot3(halves(y), const(turned_at)))))

    here(sx7.at[:, me], own_sems.at[5])
    arrived(sx7.at[:, others], recv_sems.at[2])
    prepare(sx7)
    for s in range(8):
        store_halves(0, lanes_of(s), solved[s], (2, 4), 3)
    for t in range(4):
        a = mxu(weights[1, :, 0 : 5 * total], stack[0 : 5 * total, lanes_of_pair(t)])
        b = mxu(weights[1, :, 5 * total :], stack[2 * total : 5 * total, lanes_of_pair(t)])
        ar, ai, br, bi = a[:, 0:128], a[:, 128:256], b[:, 0:128], b[:, 128:256]
        other = dot3(
            halves(jnp.concatenate([ar + bi, ai - br], axis=0)), const(coupled_at)
        )
        for r, value in enumerate((ar - bi, ai + br)):
            spread = pl.ds(2 * t + r, total, stride=8)
            flat(sums6.at[0])[spread, :] = value
            flat(sums6.at[1])[spread, :] = other[r * total : (r + 1) * total]

    def home_six(q, carry):
        send_home(
            lambda d: sums6.at[:, q, d],
            got6,
            (slice(None), q),
            10,
            home_own.at[q],
            home_recv.at[q],
        )
        return carry

    lax.fori_loop(0, block, home_six, 0)

    def tier_five(q, carry):
        got_home(got5, (chunk(q),), own_parts.at[1, q], part_sems.at[2, q])
        remote(got5.at[chunk(q)], y5.at[chunk(q)], 9, part_sems.at[3, q], (above, me)).start()
        for r in range(part):
            m = q * part + r
            back = whole(got5[m, EVEN, :], got5[m, ODD, :])
            out5[m, 0:128, :] = back[:, 0:128]
            out5[m, 128:256, :] = back[:, 128:256]
        return carry

    lax.fori_loop(0, PARTS, tier_five, 0)

    arrived(x7y, recv_sems.at[5])

    def first_mode(q):
        arrived(y5.at[chunk(q)], part_sems.at[3, q])
        for r in range(part):
            m = q * part + r
            real, imag = y5[m, EVEN, :], y5[m, ODD, :]
            wr = rates[0, pl.ds(m, 1), :]
            wi = rates[1, pl.ds(m, 1), :]
            ar, ai = x7y[m, EVEN, :] + wr * real, x7y[m, ODD, :] + wr * imag
            br, bi = wi * real, wi * imag
            z6[0, m] = jnp.concatenate([ar - bi, ai + br], axis=0)
            z6[1, m] = dot3(
                halves(jnp.concatenate([ar + bi, ai - br], axis=0)), const(coupled_at)
            )

    def tier_six(m):
        got_home(got6, (slice(None), m), home_own.at[m], home_recv.at[m])
        pair = jnp.concatenate(
            [got6[0, m, EVEN, :] + z6[0, m, 0:128], got6[0, m, ODD, :] + z6[0, m, 128:256]], axis=1
        )
        other = jnp.concatenate(
            [got6[1, m, EVEN, :] + z6[1, m, 0:128], got6[1, m, ODD, :] + z6[1, m, 128:256]], axis=1
        )
        comm = dot3(const(coupled_at), halves(pair)) - other
        real, imag = -comm[:, 128:256], comm[:, 0:128]
        damping = jnp.broadcast_to(rates[2, pl.ds(m, 1), :], (128, 128))
        inverse = 1.0 / (damping * damping + split_sq[1])
        factor_real = -damping * inverse
        factor_imag = split_sq[0] * inverse
        back = whole(
            real * factor_real - imag * factor_imag, real * factor_imag + imag * factor_real
        )
        out6[m, 0:128, :] = back[:, 0:128]
        out6[m, 128:256, :] = back[:, 128:256]

    def finish(q, carry):
        first_mode(q)
        for r in range(part):
            tier_six(q * part + r)
        return carry

    lax.fori_loop(0, PARTS, finish, 0)

    sent(tab.at[pl.ds(0, total - block)], 0)
    sent(sd6.at[:, others], 1)
    sent(sds4.at[:, :, others], 2)
    sent(sx7.at[:, others], 3)
    sent(tab, 4)
    sent(sd6, 5)
    sent(x7, 6)
    sent(m4, 7)
    sent(sums5.at[:, others], 8)
    sent(got5, 9)
    sent(sums6.at[:, :, others], 10)


def body(
    rows,
    peers,
    tier_four,
    tier_six,
    tier_seven,
    coupling,
    eigenbasis,
    energies,
    decay_rates,
    bath_coefficients,
    occupation_five,
    local_five,
    peers_five,
    places_five,
    occupation_six,
    local_six,
    peers_six,
    places_six,
):
    block = tier_four.shape[0]
    total = peers * block
    shape = tier_four.shape
    flat = (block, 256, 128)
    hbm = pl.BlockSpec(memory_space=pltpu.HBM)
    small = (
        coupling,
        eigenbasis,
        energies.reshape(1, -1),
        decay_rates.reshape(1, -1),
        bath_coefficients,
        occupation_five,
        local_five,
        peers_five.T,
        places_five.T,
        occupation_six,
        local_six,
        peers_six.T,
        places_six.T,
    )
    whole = pltpu.VMEM(flat, F32)
    pair = pltpu.VMEM((2,) + flat, F32)
    store = pltpu.VMEM((block, peers, 8, 128), F32)
    pair_store = pltpu.VMEM((2, block, peers, 8, 128), F32)
    slices = pltpu.VMEM((8, total, 128), F32)
    table = pltpu.VMEM((total, 128), F32)
    dma = pltpu.SemaphoreType.DMA
    five, six = pl.pallas_call(
        functools.partial(sweep_kernel, peers, rows, block),
        out_shape=(pltpu.VMEM(flat, F32), pltpu.VMEM(flat, F32)),
        in_specs=[hbm] * (3 + len(small)),
        scratch_shapes=[pltpu.VMEM(a.shape, a.dtype) for a in small]
        + [
            pltpu.VMEM((block, 128), F32),
            table,
            table,
            pltpu.VMEM((3,) + flat, F32),
            whole,
            pair,
            whole,
            store,
            pair_store,
            store,
            store,
            store,
            store,
            whole,
            whole,
            whole,
            pair,
            store,
            pair_store,
            slices,
            slices,
            pair,
            pltpu.VMEM((2, total, 128), F32),
            table,
            pltpu.VMEM((2, total, 8 * total), BF16),
            pltpu.VMEM((8 * total, 1024), BF16),
            pltpu.VMEM((8, 128, 128), BF16),
            pltpu.VMEM((2, 128, 256), BF16),
            pltpu.VMEM((2, 128, 128), F32),
            pltpu.VMEM((3, block, 128), F32),
            dma((11,)),
            dma((6,)),
            dma((4, PARTS)),
            dma((6,)),
            dma((2, PARTS)),
            dma((block,)),
            dma((block,)),
            dma((N_SMALL,)),
        ],
        compiler_params=pltpu.CompilerParams(
            collective_id=0, has_side_effects=True, vmem_limit_bytes=64946176
        ),
        name="sweep",
    )(
        tier_four.reshape(flat),
        tier_six.reshape(flat),
        tier_seven.reshape(flat),
        *small,
    )
    return five.reshape(shape), six.reshape(shape)


def solution(mesh):
    rows, peers = mesh.shape["ma"], mesh.shape["mb"]
    whole = P(("ma", "mb"), None, None, None)
    wide = P(("ma", "mb"), None)
    tables = (wide, P(("ma", "mb"), None, None), wide, wide)
    in_specs = (whole,) * 3 + (P(),) * 5 + tables + tables
    return jax.shard_map(
        functools.partial(body, rows, peers),
        mesh=mesh,
        in_specs=in_specs,
        out_specs=(whole, whole),
        check_vma=False,
    )
```
